256 devices in a mesh: tm: 8 (over x, core), row: 32 (over z, y).
Axes of the slice: x: 4, y: 4, z: 8, core: 2. Of those that a mesh axis runs over, the one named last changes fastest.
Arguments:
- pred_cov: bfloat16 [8, 1536, 1536], P('tm', 'row'), may hold values from -0.8 to 3.3, as said below
- cross: float32 [8, 1536, 1536], P('tm', 'row'), may hold values from -0.9 to 3.2
- filt_mean: float32 [8, 1536], P('tm', 'row'), may hold values from -6 to 6
- pred_mean: float32 [8, 1536], P('tm', 'row'), may hold values from -6 to 6
- next_smoothed: float32 [1536], P('row'), may hold values from -6 to 6
Outputs:
- smoothed: float32 [8, 1536], P('tm', 'row')
- gains: float32 [8, 1536, 1536], P('tm', 'row')
The draws below stay inside these ranges and needn't reach their ends.
Inputs may be any that keep to these rules, and one draw needn't show every extreme that they name: `pred_cov`: each of the 8 matrices of size 1536 x 1536 is symmetric positive definite.
All inputs are finite; a program needn't handle non-finite values.
Results may differ from the reference program's by a relative error of at most 0.0003.
Values may be sent and summed in bfloat16 or wider, within the bound.
No kernel may reach another device: no remote copies, remote signals or barrier semaphores. Data moves between devices by JAX's collectives and lax.ppermute only.
A program may use at most 128 MiB of HBM per device.

```python
import math
import jax
import jax.numpy as jnp
from jax import lax

MODEL_DIMENSION = 1536
HORIZON_LENGTH = 8


def shared_scales(key):
    principal_values = jax.random.uniform(jax.random.fold_in(key, 101), (HORIZON_LENGTH, MODEL_DIMENSION), jnp.float32, 1.2, 2.0)
    spans = jnp.exp(jax.random.uniform(jax.random.fold_in(key, 102), (MODEL_DIMENSION,), jnp.float32, math.log(2.0), math.log(4.0 * HORIZON_LENGTH)))
    retain_markers = jnp.exp(-1.0 / spans)
    batch_clusters = jnp.where(jax.random.uniform(jax.random.fold_in(key, 103), (HORIZON_LENGTH, MODEL_DIMENSION), jnp.float32) < 0.0625, 0.6, 1.0)
    return (principal_values, retain_markers[None, :] * batch_clusters)


def identity_mask():
    rows = lax.broadcasted_iota(jnp.int32, (MODEL_DIMENSION, MODEL_DIMENSION), 0)
    cols = lax.broadcasted_iota(jnp.int32, (MODEL_DIMENSION, MODEL_DIMENSION), 1)
    return (rows == cols)[None, :, :]


def link_coupling():
    rows = lax.broadcasted_iota(jnp.int32, (MODEL_DIMENSION, MODEL_DIMENSION), 0)
    cols = lax.broadcasted_iota(jnp.int32, (MODEL_DIMENSION, MODEL_DIMENSION), 1)
    link_spacing = jnp.abs(rows // 2 - cols // 2).astype(jnp.float32)
    wide_reach = max(MODEL_DIMENSION / 8.0, 1.0)
    kernel = 0.25 * jnp.exp(-link_spacing / 2.0) + 2.0 / wide_reach * jnp.exp(-link_spacing / wide_reach)
    same_kind = rows % 2 == cols % 2
    return jnp.where(same_kind, 1.0, -0.6) * kernel


def full_covariance(key):
    principal_values, retain_markers = shared_scales(key)
    noise = jax.random.uniform(jax.random.fold_in(key, 104), (HORIZON_LENGTH, MODEL_DIMENSION, MODEL_DIMENSION), jnp.float32, -0.5, 0.5) / MODEL_DIMENSION
    symmetric = 0.5 * (noise + jnp.swapaxes(noise, 1, 2))
    loading = jnp.exp(jax.random.uniform(jax.random.fold_in(key, 106), (HORIZON_LENGTH, MODEL_DIMENSION), jnp.float32, math.log(0.5), math.log(1.5)))
    smooth = loading[:, :, None] * loading[:, None, :] * link_coupling()[None, :, :]
    full = smooth + jnp.where(identity_mask(), principal_values[:, :, None], symmetric)
    process_share = jax.random.uniform(jax.random.fold_in(key, 107), (HORIZON_LENGTH, MODEL_DIMENSION), jnp.float32, 0.1, 0.4)
    process_noise = process_share * principal_values
    return (full, retain_markers, process_noise)


def draw_pred_cov(key, part):
    full, retain_markers, process_noise = full_covariance(key)
    return full.astype(jnp.bfloat16)


def draw_cross(key, part):
    full, retain_markers, process_noise = full_covariance(key)
    noise = jax.random.normal(jax.random.fold_in(key, 105), (HORIZON_LENGTH, MODEL_DIMENSION, MODEL_DIMENSION), jnp.float32) * 0.01
    reduced = full - jnp.where(identity_mask(), process_noise[:, :, None], 0.0)
    return retain_markers[:, :, None] * reduced + noise


def draw_pred_mean(key, part):
    values = jax.random.normal(jax.random.fold_in(key, 201), (HORIZON_LENGTH, MODEL_DIMENSION), jnp.float32)
    return jnp.clip(values, -6.0, 6.0)


def block_levels(rng, shape, pieces, smallest, high):
    loudness, own = 1.0, jax.random.fold_in(rng, 6)
    for dim, shards_of in pieces:
        draws = jnp.exp(jax.random.uniform(jax.random.fold_in(own, dim), (shards_of,), jnp.float32, smallest / len(pieces), high / len(pieces)))
        loudness = loudness * jnp.repeat(draws, shape[dim] // shards_of).reshape([-1 if axis == dim else 1 for axis in range(len(shape))])
    return loudness


def bell_draw(stream_key, dims, spread, limit, pieces=(), kind=jnp.bfloat16):
    entries = spread * jax.random.normal(stream_key, dims, jnp.float32)
    if pieces:
        entries = entries * block_levels(stream_key, dims, pieces, -0.22, 0.18)
    return jnp.clip(entries, -limit, limit).astype(kind)


def setup_inputs(seed: int = 0) -> dict:
    arg_keys = jax.random.split(jax.random.key(seed), 6)
    pred_cov = draw_pred_cov(jax.random.fold_in(arg_keys[5], 71), 0)
    cross = draw_cross(jax.random.fold_in(arg_keys[5], 71), 0)
    filt_mean = bell_draw(arg_keys[2], (HORIZON_LENGTH, MODEL_DIMENSION), 1.0, 6.0, ((0, 8), (1, 32)), jnp.float32)
    pred_mean = draw_pred_mean(jax.random.fold_in(arg_keys[5], 71), 0)
    next_smoothed = bell_draw(arg_keys[4], (MODEL_DIMENSION,), 1.0, 6.0, ((0, 32),), jnp.float32)
    return dict(pred_cov=pred_cov, cross=cross, filt_mean=filt_mean, pred_mean=pred_mean, next_smoothed=next_smoothed)


def one_gain(pair):
    cov, part = pair
    cholesky_factor = jnp.linalg.cholesky(cov.astype(jnp.float32))
    return jax.scipy.linalg.cho_solve((cholesky_factor, True), part.T).T

def reference(pred_cov, cross, filt_mean, pred_mean, next_smoothed):
    gains = lax.map(one_gain, (pred_cov, cross))

    def backward(later, items):
        gain, mean_f, mean_p = items
        now = mean_f + jnp.dot(gain.astype(jnp.float32), (later - mean_p).astype(jnp.float32), precision=lax.Precision.HIGHEST, preferred_element_type=jnp.float32)
        return (now, now)
    _, smoothed = lax.scan(backward, next_smoothed, (gains, filt_mean, pred_mean), reverse=True)
    return (smoothed, gains)
```

```python
import jax
import jax.numpy as jnp
from jax import lax
from jax.experimental import pallas as pl
from jax.experimental.pallas import tpu as pltpu
from jax.sharding import PartitionSpec as P

f32, bf16 = jnp.float32, jnp.bfloat16
N, B, H, LANES = 1536, 256, 128, 128
NB = N // B
VMEM_WHOLE = pl.BlockSpec(memory_space=pltpu.VMEM)

def inv4(d):
    a,b,c=d[0][0],d[1][0],d[1][1]
    r=1.0/(a*c-b*b)
    p,q,s=c*r,-b*r,a*r
    e0,e1,g0,g1=d[2][0],d[2][1],d[3][0],d[3][1]
    x00,x01=e0*p+e1*q,e0*q+e1*s
    x10,x11=g0*p+g1*q,g0*q+g1*s
    u=d[2][2]-(x00*e0+x01*e1)
    v=d[3][2]-(x10*e0+x11*e1)
    w=d[3][3]-(x10*g0+x11*g1)
    r2=1.0/(u*w-v*v)
    U,V,W=w*r2,-v*r2,u*r2
    y00,y01=U*x00+V*x10,U*x01+V*x11
    y10,y11=V*x00+W*x10,V*x01+W*x11
    i00=p+x00*y00+x10*y10
    i01=q+x00*y01+x10*y11
    i11=s+x01*y01+x11*y11
    return [[i00,i01,-y00,-y10],[i01,i11,-y01,-y11],[-y00,-y01,U,V],[-y10,-y11,V,W]]

def leaf(m_ref, K=4):
    n=m_ref.shape[0]
    lane=lax.broadcasted_iota(jnp.int32,(1,n),1)
    lanef=lax.broadcasted_iota(jnp.int32,(n,n),1)
    for p0 in range(0,n,K):
        M=m_ref[...]
        c=[jnp.broadcast_to(M[:,p0+q:p0+q+1],(n,n)) for q in range(K)]
        d=[[c[j][p0+i:p0+i+1,:] for j in range(i+1)] for i in range(K)]
        Di=inv4(d)
        r=[M[p0+q:p0+q+1,:] for q in range(K)]
        t=[]
        for i in range(K):
            x=Di[i][0]*r[0]
            for j in range(1,K): x=x+Di[i][j]*r[j]
            for j in range(K): x=jnp.where(lane==p0+j,-Di[i][j],x)
            t.append(x)
        new=jnp.where((lanef>=p0)&(lanef<p0+K),0.0,M)
        for q in range(K): new=new-c[q]*t[q]
        m_ref[...]=new
        m_ref[p0:p0+K,:]=jnp.concatenate(t,0)

def split(x):
    h=x.astype(bf16); return h,(x-h.astype(f32)).astype(bf16)

def dot3(a,b):
    ah,al=split(a); bh,bl=split(b)
    return jnp.dot(jnp.concatenate([ah,ah,al],1),jnp.concatenate([bh,bl,bh],0),preferred_element_type=f32)

def kern(p_ref,c_ref,w_ref,g_ref,m_ref,di_ref,t3_ref,c3_ref,cd_ref):
    w_ref[...]=p_ref[...].astype(f32)
    def step(k,_):
        o=pl.multiple_of(k*B,B)
        D=w_ref.at[pl.ds(o,B),pl.ds(o,B)]
        m_ref[...]=D[:H,:H]; leaf(m_ref); ai=-m_ref[...]
        b=D[:H,H:]; bt=D[H:,:H]
        X=dot3(ai,b); Xt=dot3(bt,ai)
        m_ref[...]=D[H:,H:]-dot3(bt,X)
        leaf(m_ref); si=-m_ref[...]
        XS=dot3(X,si)
        di_ref[:H,:H]=ai+dot3(XS,Xt)
        di_ref[:H,H:]=-XS
        di_ref[H:,:H]=-dot3(si,Xt)
        di_ref[H:,H:]=si
        di=di_ref[...]
        R=w_ref[pl.ds(o,B),:]
        T=dot3(di,R)
        h,l=split(T)
        t3_ref[:B,:]=h; t3_ref[B:2*B,:]=l; t3_ref[2*B:,:]=h
        C=w_ref[:,pl.ds(o,B)]
        h,l=split(C)
        c3_ref[:,:B]=h; c3_ref[:,B:2*B]=h; c3_ref[:,2*B:]=l
        dh,dl=split(di)
        d3=jnp.concatenate([dh,dl,dh],0)
        def cdl(i,_):
            q=pl.multiple_of(i*B,B)
            cd_ref[pl.ds(q,B),:]=jnp.dot(c3_ref[pl.ds(q,B),:],d3,preferred_element_type=f32)
            return 0
        lax.fori_loop(0,NB,cdl,0)
        def upd(i,_):
            q=pl.multiple_of(i*B,B)
            w_ref[pl.ds(q,B),:]=w_ref[pl.ds(q,B),:]-jnp.dot(c3_ref[pl.ds(q,B),:],t3_ref[...],preferred_element_type=f32)
            return 0
        lax.fori_loop(0,NB,upd,0)
        w_ref[pl.ds(o,B),:]=T
        w_ref[:,pl.ds(o,B)]=cd_ref[...]
        w_ref[pl.ds(o,B),pl.ds(o,B)]=-di
        return 0
    lax.fori_loop(0,NB,step,0)
    c=c_ref[...]
    ch,cl=split(c)
    c3=jnp.concatenate([ch,ch,cl],1)
    def gains(j,_):
        q=pl.multiple_of(j*B,B)
        wh,wl=split(w_ref[:,pl.ds(q,B)])
        g_ref[:,pl.ds(q,B)]=-jnp.dot(c3,jnp.concatenate([wh,wl,wh],0),preferred_element_type=f32)
        return 0
    lax.fori_loop(0,NB,gains,0)

def inverse(p,c):
    return pl.pallas_call(kern,out_shape=[jax.ShapeDtypeStruct((N,N),f32),jax.ShapeDtypeStruct(c.shape,f32)],
      in_specs=[pl.BlockSpec(memory_space=pltpu.VMEM)]*2,out_specs=[pl.BlockSpec(memory_space=pltpu.VMEM)]*2,
      scratch_shapes=[pltpu.VMEM((H,H),f32),pltpu.VMEM((B,B),f32),pltpu.VMEM((3*B,N),bf16),pltpu.VMEM((N,3*B),bf16),pltpu.VMEM((N,B),f32)],
      compiler_params=pltpu.CompilerParams(vmem_limit_bytes=26<<20))(p,c)

def vectors_kernel(x_ref, o_ref):
    for j in range(N // LANES):
        rows = slice(j * LANES, (j + 1) * LANES)
        o_ref[:, rows] = x_ref[rows, :].T[:8, :]


def vectors(packed):
    return pl.pallas_call(
        vectors_kernel,
        out_shape=jax.ShapeDtypeStruct((8, N), f32),
        grid=(1,),
        in_specs=[pl.BlockSpec((N, LANES), lambda i: (0, N // LANES))],
        out_specs=pl.BlockSpec((8, N), lambda i: (0, 0)),
        compiler_params=pltpu.CompilerParams(vmem_limit_bytes=4 << 20),
    )(packed)


def matvec(m_ref, v, out_ref):
    for i in range(N // LANES):
        rows = slice(i * LANES, (i + 1) * LANES)
        total = m_ref[rows, :LANES] * v[:, :LANES]
        for j in range(1, N // LANES):
            lanes = slice(j * LANES, (j + 1) * LANES)
            total = total + m_ref[rows, lanes] * v[:, lanes]
        out_ref[:, rows] = jnp.sum(total.T, axis=0, keepdims=True)


def turn_kernel(late_ref, base_ref, mean_ref, w_ref, c_ref, s_ref, y_ref):
    matvec(w_ref, late_ref[...] + base_ref[...], y_ref)
    matvec(c_ref, y_ref[...], s_ref)
    s_ref[...] = mean_ref[...] - s_ref[...]


def turn(late, base, mean, minus_inverse, packed):
    return pl.pallas_call(
        turn_kernel,
        out_shape=jax.ShapeDtypeStruct((1, N), f32),
        in_specs=[VMEM_WHOLE] * 5,
        out_specs=VMEM_WHOLE,
        scratch_shapes=[pltpu.VMEM((1, N), f32)],
        compiler_params=pltpu.CompilerParams(vmem_limit_bytes=4 << 20),
        cost_estimate=pl.CostEstimate(flops=4 * N * N, bytes_accessed=8 * N * N, transcendentals=0),
    )(late, base, mean, minus_inverse, packed)


def per_device(pred_cov, cross, filt_mean, pred_mean, next_smoothed):
    steps = lax.axis_size("tm")
    row = lax.axis_index("row")
    mine = cross.shape[1]
    whole_cov = lax.all_gather(pred_cov[0], "row", axis=0, tiled=True)
    columns = jnp.stack([filt_mean[0], pred_mean[0], next_smoothed], axis=1)
    packed = jnp.concatenate([cross[0], jnp.pad(columns, ((0, 0), (0, LANES - 3)))], axis=1)
    packed = lax.all_gather(packed, "row", axis=0, tiled=True)
    minus_inverse, gain = inverse(whole_cov, cross[0])
    rows = vectors(packed)
    mean = rows[0:1]
    final = lax.axis_index("tm") == steps - 1
    base = jnp.where(final, rows[2:3], 0.0) - rows[1:2]
    state = turn(jnp.zeros_like(mean), base, mean, minus_inverse, packed)
    for _ in range(steps - 1):
        late = lax.ppermute(state, "tm", [(i, i - 1) for i in range(1, steps)])
        state = turn(late, base, mean, minus_inverse, packed)
    smoothed = lax.dynamic_slice(state[0], (row * mine,), (mine,))
    return (smoothed[None, :], gain[None, :, :])


def solution(mesh):
    in_specs = (
        P("tm", "row", None),
        P("tm", "row", None),
        P("tm", "row"),
        P("tm", "row"),
        P("row"),
    )
    out_specs = (P("tm", "row"), P("tm", "row", None))
    return jax.shard_map(
        per_device, mesh=mesh, in_specs=in_specs, out_specs=out_specs, check_vma=False
    )
```

```python
import functools

import jax
import jax.numpy as jnp
from jax import lax
from jax.experimental import pallas as pl
from jax.experimental.pallas import tpu as pltpu
from jax.sharding import PartitionSpec as P

f32, bf16 = jnp.float32, jnp.bfloat16
N, LANES = 1536, 128
MINE = 48
PIECE = 4 * MINE
B = 2 * PIECE
H = 128
TILE = 512
Y, Z = 4, 8
VMEM_WHOLE = pl.BlockSpec(memory_space=pltpu.VMEM)
SMEM_WHOLE = pl.BlockSpec(memory_space=pltpu.SMEM)

def inv4(d):
    a,b,c=d[0][0],d[1][0],d[1][1]
    r=1.0/(a*c-b*b)
    p,q,s=c*r,-b*r,a*r
    e0,e1,g0,g1=d[2][0],d[2][1],d[3][0],d[3][1]
    x00,x01=e0*p+e1*q,e0*q+e1*s
    x10,x11=g0*p+g1*q,g0*q+g1*s
    u=d[2][2]-(x00*e0+x01*e1)
    v=d[3][2]-(x10*e0+x11*e1)
    w=d[3][3]-(x10*g0+x11*g1)
    r2=1.0/(u*w-v*v)
    U,V,W=w*r2,-v*r2,u*r2
    y00,y01=U*x00+V*x10,U*x01+V*x11
    y10,y11=V*x00+W*x10,V*x01+W*x11
    i00=p+x00*y00+x10*y10
    i01=q+x00*y01+x10*y11
    i11=s+x01*y01+x11*y11
    return [[i00,i01,-y00,-y10],[i01,i11,-y01,-y11],[-y00,-y01,U,V],[-y10,-y11,V,W]]

def leaf(m_ref, K=4):
    n=m_ref.shape[0]
    lane=lax.broadcasted_iota(jnp.int32,(1,n),1)
    lanef=lax.broadcasted_iota(jnp.int32,(n,n),1)
    for p0 in range(0,n,K):
        M=m_ref[...]
        c=[jnp.broadcast_to(M[:,p0+q:p0+q+1],(n,n)) for q in range(K)]
        d=[[c[j][p0+i:p0+i+1,:] for j in range(i+1)] for i in range(K)]
        Di=inv4(d)
        r=[M[p0+q:p0+q+1,:] for q in range(K)]
        t=[]
        for i in range(K):
            x=Di[i][0]*r[0]
            for j in range(1,K): x=x+Di[i][j]*r[j]
            for j in range(K): x=jnp.where(lane==p0+j,-Di[i][j],x)
            t.append(x)
        new=jnp.where((lanef>=p0)&(lanef<p0+K),0.0,M)
        for q in range(K): new=new-c[q]*t[q]
        m_ref[...]=new
        m_ref[p0:p0+K,:]=jnp.concatenate(t,0)


def split(x):
    h = x.astype(bf16)
    return h, (x - h.astype(f32)).astype(bf16)


def wide(x):
    h, l = split(x)
    return jnp.concatenate([h, h, l], 1)


def tall(x):
    h, l = split(x)
    return jnp.concatenate([h, l, h], 0)


def dot(a, b):
    return jnp.dot(a, b, preferred_element_type=f32)


def block_sweep(d_ref, m_ref, r_ref):
    def step(k, _):
        o = pl.multiple_of(k * H, H)
        m_ref[...] = d_ref[pl.ds(o, H), pl.ds(o, H)]
        leaf(m_ref)
        minus = m_ref[...]
        t = -dot(wide(minus), tall(d_ref[pl.ds(o, H), :]))
        c = wide(d_ref[:, pl.ds(o, H)])
        r_ref[...] = -dot(c, tall(minus))
        d_ref[...] = d_ref[...] - dot(c, tall(t))
        d_ref[pl.ds(o, H), :] = t
        d_ref[:, pl.ds(o, H)] = r_ref[...]
        d_ref[pl.ds(o, H), pl.ds(o, H)] = minus
        return 0

    lax.fori_loop(0, B // H, step, 0)


def stage_kernel(stage, ids, near_ref, far_ref, *refs):
    if stage:
        _, *refs = refs
    if stage == N // B - 1:
        cross_ref, *refs = refs
        w_ref, g_ref, p_ref, t3_ref, d_ref, m_ref, r_ref = refs
    else:
        w_ref, p_ref, t3_ref, d_ref, m_ref, r_ref = refs
    here = pl.multiple_of(ids[stage] * B, B)
    for n, ref in enumerate((near_ref, far_ref)):
        z = ids[4 + n]
        for d in range(Y):
            y = lax.rem(ids[6] + d, Y)
            to = pl.multiple_of(lax.rem(z, 2) * PIECE + y * MINE, 16)
            p_ref[pl.ds(to, MINE), :] = ref[d * MINE : (d + 1) * MINE, :]
    rows = pl.ds(here, B)
    w_ref[rows, :] = p_ref[...].astype(f32)
    if stage:

        def clear(j, _):
            w_ref[rows, pl.ds(pl.multiple_of(ids[j] * B, B), B)] = jnp.zeros((B, B), f32)
            return 0

        lax.fori_loop(0, stage, clear, 0)

        def earlier(j, _):
            there = pl.multiple_of(ids[j] * B, B)
            p = p_ref[:, pl.ds(there, B)]
            p = jnp.concatenate([p, p], 1)

            def tile(n, _):
                q = pl.ds(pl.multiple_of(n * TILE, TILE), TILE)
                h, l = split(w_ref[pl.ds(there, B), q])
                w_ref[rows, q] = w_ref[rows, q] - dot(p, jnp.concatenate([h, l], 0))
                return 0

            return lax.fori_loop(0, N // TILE, tile, 0)

        lax.fori_loop(0, stage, earlier, 0)
    d_ref[...] = w_ref[rows, pl.ds(here, B)]
    block_sweep(d_ref, m_ref, r_ref)
    minus = d_ref[...]
    left = wide(minus)

    def forward(n, _):
        q = pl.ds(pl.multiple_of(n * TILE, TILE), TILE)
        t = -dot(left, tall(w_ref[rows, q]))
        t3_ref[:, q] = tall(t)
        w_ref[rows, q] = t
        return 0

    lax.fori_loop(0, N // TILE, forward, 0)
    w_ref[rows, pl.ds(here, B)] = minus
    if stage:

        def update(j, _):
            back = pl.ds(pl.multiple_of(ids[j] * B, B), B)
            c = wide(w_ref[back, pl.ds(here, B)])
            d_ref[...] = -dot(c, tall(minus))

            def tile(n, _):
                q = pl.ds(pl.multiple_of(n * TILE, TILE), TILE)
                w_ref[back, q] = w_ref[back, q] - dot(c, t3_ref[:, q])
                return 0

            lax.fori_loop(0, N // TILE, tile, 0)
            w_ref[back, pl.ds(here, B)] = d_ref[...]
            return 0

        lax.fori_loop(0, stage, update, 0)
    if stage == N // B - 1:
        c3 = wide(cross_ref[...])

        def gains(j, _):
            q = pl.ds(pl.multiple_of(j * B, B), B)
            g_ref[:, q] = -dot(c3, tall(w_ref[:, q]))
            return 0

        lax.fori_loop(0, N // B, gains, 0)


def sweep_stage(stage, ids, near, far, w, cross):
    last = stage == N // B - 1
    args = [ids, near, far] + ([w] if stage else []) + ([cross] if last else [])
    out = [pltpu.VMEM((N, N), f32)] + ([jax.ShapeDtypeStruct(cross.shape, f32)] if last else [])
    return pl.pallas_call(
        functools.partial(stage_kernel, stage),
        name="stage" + str(stage),
        out_shape=out,
        in_specs=[SMEM_WHOLE] + [VMEM_WHOLE] * (len(args) - 1),
        out_specs=[VMEM_WHOLE] * len(out),
        scratch_shapes=[
            pltpu.VMEM((B, N), bf16),
            pltpu.VMEM((3 * B, N), bf16),
            pltpu.VMEM((B, B), f32),
            pltpu.VMEM((H, H), f32),
            pltpu.VMEM((B, H), f32),
        ],
        input_output_aliases={3: 0} if stage else {},
        compiler_params=pltpu.CompilerParams(vmem_limit_bytes=STAGE_VMEM),
        cost_estimate=pl.CostEstimate(flops=40_000_000_000, bytes_accessed=4 * B * N, transcendentals=0),
    )(*args)


STAGE_VMEM = 24 << 20


def matvec(m_ref, v, out_ref):
    def block(i, _):
        rows = pl.ds(pl.multiple_of(i * LANES, LANES), LANES)
        total = m_ref[rows, :LANES] * v[:, :LANES]
        for j in range(1, N // LANES):
            lanes = slice(j * LANES, (j + 1) * LANES)
            total = total + m_ref[rows, lanes] * v[:, lanes]
        out_ref[:, rows] = jnp.sum(total.T, axis=0, keepdims=True)
        return 0

    lax.fori_loop(0, N // LANES, block, 0)


def turn_kernel(late_ref, base_ref, mean_ref, w_ref, c_ref, s_ref, y_ref):
    matvec(w_ref, late_ref[...] + base_ref[...], y_ref)
    matvec(c_ref, y_ref[...], s_ref)
    s_ref[...] = mean_ref[...] - s_ref[...]


def turn(late, base, mean, minus_inverse, packed):
    return pl.pallas_call(
        turn_kernel,
        out_shape=jax.ShapeDtypeStruct((1, N), f32),
        in_specs=[VMEM_WHOLE] * 5,
        out_specs=VMEM_WHOLE,
        scratch_shapes=[pltpu.VMEM((1, N), f32)],
        compiler_params=pltpu.CompilerParams(vmem_limit_bytes=4 << 20),
        cost_estimate=pl.CostEstimate(flops=4 * N * N, bytes_accessed=8 * N * N, transcendentals=0),
    )(late, base, mean, minus_inverse, packed)


def first_kernel(final_ref, w_ref, x_ref, s_ref, base_ref, mean_ref, y_ref):
    for j in range(N // LANES):
        rows = slice(j * LANES, (j + 1) * LANES)
        vectors = x_ref[rows, N:].T[:8, :]
        mean_ref[:, rows] = vectors[0:1]
        base_ref[:, rows] = jnp.where(final_ref[0] > 0, vectors[2:3], 0.0) - vectors[1:2]
    matvec(w_ref, base_ref[...], y_ref)
    matvec(x_ref, y_ref[...], s_ref)
    s_ref[...] = mean_ref[...] - s_ref[...]


def first_turn(final, minus_inverse, packed):
    return pl.pallas_call(
        first_kernel,
        out_shape=[jax.ShapeDtypeStruct((1, N), f32)] * 3,
        in_specs=[SMEM_WHOLE] + [VMEM_WHOLE] * 2,
        out_specs=[VMEM_WHOLE] * 3,
        scratch_shapes=[pltpu.VMEM((1, N), f32)],
        compiler_params=pltpu.CompilerParams(vmem_limit_bytes=4 << 20),
        cost_estimate=pl.CostEstimate(flops=4 * N * N, bytes_accessed=8 * N * N, transcendentals=0),
    )(final, minus_inverse, packed)


def swap(x, inner):
    pairs = []
    for z in range(Z):
        other = z ^ 1 if inner else (z + (1 if z % 2 else -1)) % Z
        pairs += [(z * Y + y, other * Y + y) for y in range(Y)]
    return lax.ppermute(x, "row", pairs)


def along_y(x, d):
    return lax.ppermute(x, "row", [(z * Y + (y + d) % Y, z * Y + y) for z in range(Z) for y in range(Y)])


def per_device(pred_cov, cross, filt_mean, pred_mean, next_smoothed):
    steps = lax.axis_size("tm")
    row = lax.axis_index("row")
    y, z = row % Y, row // Y
    columns = jnp.stack([filt_mean[0], pred_mean[0], next_smoothed], axis=1)
    packed = jnp.concatenate([cross[0], jnp.pad(columns, ((0, 0), (0, LANES - 3)))], axis=1)
    packed = lax.all_gather(packed, "row", axis=0, tiled=True)

    own = jnp.concatenate([pred_cov[0]] + [along_y(pred_cov[0], d) for d in range(1, Y)], axis=0)
    a1, b1 = swap(own, True), swap(own, False)
    a2, b2 = swap(b1, True), swap(a1, False)
    a3, b3 = swap(b2, True), swap(a2, False)
    b4 = swap(a3, False)
    e = 1 - 2 * (z % 2)
    at = lambda k: (z + e * k + Z) % Z
    order = [at(0) // 2, at(-1) // 2, at(2) // 2, at(-3) // 2]
    ids = lambda m, n: jnp.stack(order + [at(m), at(n), y, y]).astype(jnp.int32)
    w = sweep_stage(0, ids(0, 1), own, a1, None, None)[0]
    w = sweep_stage(1, ids(-1, -2), b1, b2, w, None)[0]
    w = sweep_stage(2, ids(2, 3), a2, a3, w, None)[0]
    minus_inverse, gain = sweep_stage(3, ids(-3, -4), b3, b4, w, cross[0])

    final = lax.axis_index("tm") == steps - 1
    state, base, mean = first_turn(final.astype(f32)[None], minus_inverse, packed)
    for _ in range(steps - 1):
        late = lax.ppermute(state, "tm", [(i, i - 1) for i in range(1, steps)])
        state = turn(late, base, mean, minus_inverse, packed)
    smoothed = lax.dynamic_slice(state[0], (row * MINE,), (MINE,))
    return (smoothed[None, :], gain[None, :, :])


def solution(mesh):
    in_specs = (
        P("tm", "row", None),
        P("tm", "row", None),
        P("tm", "row"),
        P("tm", "row"),
        P("row"),
    )
    out_specs = (P("tm", "row"), P("tm", "row", None))
    return jax.shard_map(
        per_device, mesh=mesh, in_specs=in_specs, out_specs=out_specs, check_vma=False
    )
```

```python
import functools

import jax
import jax.numpy as jnp
from jax import lax
from jax.experimental import pallas as pl
from jax.experimental.pallas import tpu as pltpu
from jax.sharding import PartitionSpec as P

f32, bf16 = jnp.float32, jnp.bfloat16
N, LANES = 1536, 128
MINE = 48
PIECE = 4 * MINE
B = 2 * PIECE
H = 128
TILE = 512
Y, Z = 4, 8
VMEM_WHOLE = pl.BlockSpec(memory_space=pltpu.VMEM)
SMEM_WHOLE = pl.BlockSpec(memory_space=pltpu.SMEM)

def inv4(d):
    a,b,c=d[0][0],d[1][0],d[1][1]
    r=1.0/(a*c-b*b)
    p,q,s=c*r,-b*r,a*r
    e0,e1,g0,g1=d[2][0],d[2][1],d[3][0],d[3][1]
    x00,x01=e0*p+e1*q,e0*q+e1*s
    x10,x11=g0*p+g1*q,g0*q+g1*s
    u=d[2][2]-(x00*e0+x01*e1)
    v=d[3][2]-(x10*e0+x11*e1)
    w=d[3][3]-(x10*g0+x11*g1)
    r2=1.0/(u*w-v*v)
    U,V,W=w*r2,-v*r2,u*r2
    y00,y01=U*x00+V*x10,U*x01+V*x11
    y10,y11=V*x00+W*x10,V*x01+W*x11
    i00=p+x00*y00+x10*y10
    i01=q+x00*y01+x10*y11
    i11=s+x01*y01+x11*y11
    return [[i00,i01,-y00,-y10],[i01,i11,-y01,-y11],[-y00,-y01,U,V],[-y10,-y11,V,W]]

def leaf(m_ref, K=4):
    n=m_ref.shape[0]
    lane=lax.broadcasted_iota(jnp.int32,(1,n),1)
    lanef=lax.broadcasted_iota(jnp.int32,(n,n),1)
    for p0 in range(0,n,K):
        M=m_ref[...]
        c=[jnp.broadcast_to(M[:,p0+q:p0+q+1],(n,n)) for q in range(K)]
        d=[[c[j][p0+i:p0+i+1,:] for j in range(i+1)] for i in range(K)]
        Di=inv4(d)
        r=[M[p0+q:p0+q+1,:] for q in range(K)]
        t=[]
        for i in range(K):
            x=Di[i][0]*r[0]
            for j in range(1,K): x=x+Di[i][j]*r[j]
            for j in range(K): x=jnp.where(lane==p0+j,-Di[i][j],x)
            t.append(x)
        new=jnp.where((lanef>=p0)&(lanef<p0+K),0.0,M)
        for q in range(K): new=new-c[q]*t[q]
        m_ref[...]=new
        m_ref[p0:p0+K,:]=jnp.concatenate(t,0)


def split(x):
    h = x.astype(bf16)
    return h, (x - h.astype(f32)).astype(bf16)


def wide(x):
    h, l = split(x)
    return jnp.concatenate([h, h, l], 1)


def tall(x):
    h, l = split(x)
    return jnp.concatenate([h, l, h], 0)


def dot(a, b):
    return jnp.dot(a, b, preferred_element_type=f32)


def block_sweep(d_ref, m_ref, r_ref):
    def step(k, _):
        o = pl.multiple_of(k * H, H)
        m_ref[...] = d_ref[pl.ds(o, H), pl.ds(o, H)]
        leaf(m_ref)
        minus = m_ref[...]
        t = -dot(wide(minus), tall(d_ref[pl.ds(o, H), :]))
        c = wide(d_ref[:, pl.ds(o, H)])
        r_ref[...] = -dot(c, tall(minus))
        d_ref[...] = d_ref[...] - dot(c, tall(t))
        d_ref[pl.ds(o, H), :] = t
        d_ref[:, pl.ds(o, H)] = r_ref[...]
        d_ref[pl.ds(o, H), pl.ds(o, H)] = minus
        return 0

    lax.fori_loop(0, B // H, step, 0)


def stage_kernel(stage, ids, near_ref, far_ref, *refs):
    if stage:
        _, *refs = refs
    if stage == N // B - 1:
        cross_ref, *refs = refs
        w_ref, g_ref, p_ref, t3_ref, d_ref, m_ref, r_ref = refs
    else:
        w_ref, p_ref, t3_ref, d_ref, m_ref, r_ref = refs
    here = pl.multiple_of(ids[stage] * B, B)
    for n, ref in enumerate((near_ref, far_ref)):
        z = ids[4 + n]
        for d in range(Y):
            y = lax.rem(ids[6] + d, Y)
            to = pl.multiple_of(lax.rem(z, 2) * PIECE + y * MINE, 16)
            p_ref[pl.ds(to, MINE), :] = ref[d * MINE : (d + 1) * MINE, :]
    rows = pl.ds(here, B)
    w_ref[rows, :] = p_ref[...].astype(f32)
    if stage:

        def clear(j, _):
            w_ref[rows, pl.ds(pl.multiple_of(ids[j] * B, B), B)] = jnp.zeros((B, B), f32)
            return 0

        lax.fori_loop(0, stage, clear, 0)

        def earlier(j, _):
            there = pl.multiple_of(ids[j] * B, B)
            p = p_ref[:, pl.ds(there, B)]
            p = jnp.concatenate([p, p], 1)

            def tile(n, _):
                q = pl.ds(pl.multiple_of(n * TILE, TILE), TILE)
                h, l = split(w_ref[pl.ds(there, B), q])
                w_ref[rows, q] = w_ref[rows, q] - dot(p, jnp.concatenate([h, l], 0))
                return 0

            return lax.fori_loop(0, N // TILE, tile, 0)

        lax.fori_loop(0, stage, earlier, 0)
    d_ref[...] = w_ref[rows, pl.ds(here, B)]
    block_sweep(d_ref, m_ref, r_ref)
    minus = d_ref[...]
    left = wide(minus)

    def forward(n, _):
        q = pl.ds(pl.multiple_of(n * TILE, TILE), TILE)
        t = -dot(left, tall(w_ref[rows, q]))
        t3_ref[:, q] = tall(t)
        w_ref[rows, q] = t
        return 0

    lax.fori_loop(0, N // TILE, forward, 0)
    w_ref[rows, pl.ds(here, B)] = minus
    if stage:

        def update(j, _):
            back = pl.ds(pl.multiple_of(ids[j] * B, B), B)
            c = wide(w_ref[back, pl.ds(here, B)])
            d_ref[...] = -dot(c, tall(minus))

            def tile(n, _):
                q = pl.ds(pl.multiple_of(n * TILE, TILE), TILE)
                w_ref[back, q] = w_ref[back, q] - dot(c, t3_ref[:, q])
                return 0

            lax.fori_loop(0, N // TILE, tile, 0)
            w_ref[back, pl.ds(here, B)] = d_ref[...]
            return 0

        lax.fori_loop(0, stage, update, 0)
    if stage == N // B - 1:
        c3 = wide(cross_ref[...])

        def gains(j, _):
            q = pl.ds(pl.multiple_of(j * B, B), B)
            g_ref[:, q] = -dot(c3, tall(w_ref[:, q]))
            return 0

        lax.fori_loop(0, N // B, gains, 0)


def sweep_stage(stage, ids, near, far, w, cross):
    last = stage == N // B - 1
    args = [ids, near, far] + ([w] if stage else []) + ([cross] if last else [])
    out = [pltpu.VMEM((N, N), f32)] + ([jax.ShapeDtypeStruct(cross.shape, f32)] if last else [])
    return pl.pallas_call(
        functools.partial(stage_kernel, stage),
        name="stage" + str(stage),
        out_shape=out,
        in_specs=[SMEM_WHOLE] + [VMEM_WHOLE] * (len(args) - 1),
        out_specs=[VMEM_WHOLE] * len(out),
        scratch_shapes=[
            pltpu.VMEM((B, N), bf16),
            pltpu.VMEM((3 * B, N), bf16),
            pltpu.VMEM((B, B), f32),
            pltpu.VMEM((H, H), f32),
            pltpu.VMEM((B, H), f32),
        ],
        input_output_aliases={3: 0} if stage else {},
        compiler_params=pltpu.CompilerParams(vmem_limit_bytes=STAGE_VMEM),
        cost_estimate=pl.CostEstimate(flops=40_000_000_000, bytes_accessed=4 * B * N, transcendentals=0),
    )(*args)


STAGE_VMEM = 24 << 20


def matvec(m_ref, v_ref, out_ref, part_ref):
    def block(i, _):
        rows = pl.ds(pl.multiple_of(i * LANES, LANES), LANES)
        total = m_ref[rows, :LANES] * v_ref[:, :LANES]
        for j in range(1, N // LANES):
            lanes = slice(j * LANES, (j + 1) * LANES)
            total = total + m_ref[rows, lanes] * v_ref[:, lanes]
        part_ref[rows, :] = total
        return 0

    lax.fori_loop(0, N // LANES, block, 0)
    for i in range(N // LANES):
        rows = slice(i * LANES, (i + 1) * LANES)
        out_ref[:, rows] = jnp.sum(part_ref[rows, :].T, axis=0, keepdims=True)


def turn_kernel(n, mine_ref, *refs):
    if n:
        late_ref, before_ref, base_ref, mean_ref, w_ref, x_ref, s_ref, v_ref, y_ref, part_ref = refs
    else:
        w_ref, x_ref, s_ref, base_ref, mean_ref, v_ref, y_ref, part_ref = refs
        for j in range(N // LANES):
            rows = slice(j * LANES, (j + 1) * LANES)
            vectors = x_ref[rows, N:].T[:8, :]
            mean_ref[:, rows] = vectors[0:1]
            base_ref[:, rows] = jnp.where(mine_ref[0] == 0, vectors[2:3], 0.0) - vectors[1:2]

    @pl.when(mine_ref[0] == n)
    def _():
        v_ref[...] = late_ref[...] + base_ref[...] if n else base_ref[...]
        matvec(w_ref, v_ref, y_ref, part_ref)
        matvec(x_ref, y_ref, s_ref, part_ref)
        s_ref[...] = mean_ref[...] - s_ref[...]

    @pl.when(mine_ref[0] != n)
    def _():
        s_ref[...] = before_ref[...] if n else mean_ref[...]


def turn(n, mine, *args):
    return pl.pallas_call(
        functools.partial(turn_kernel, n),
        name="turn" + str(n),
        out_shape=[jax.ShapeDtypeStruct((1, N), f32)] * (1 if n else 3),
        in_specs=[SMEM_WHOLE] + [VMEM_WHOLE] * len(args),
        out_specs=[VMEM_WHOLE] * (1 if n else 3),
        scratch_shapes=[pltpu.VMEM((1, N), f32), pltpu.VMEM((1, N), f32), pltpu.VMEM((N, LANES), f32)],
        compiler_params=pltpu.CompilerParams(vmem_limit_bytes=4 << 20),
        cost_estimate=pl.CostEstimate(flops=4 * N * N, bytes_accessed=8 * N * N, transcendentals=0),
    )(mine, *args)


def swap(x, inner):
    pairs = []
    for z in range(Z):
        other = z ^ 1 if inner else (z + (1 if z % 2 else -1)) % Z
        pairs += [(z * Y + y, other * Y + y) for y in range(Y)]
    return lax.ppermute(x, "row", pairs)


def along_y(x, d):
    return lax.ppermute(x, "row", [(z * Y + (y + d) % Y, z * Y + y) for z in range(Z) for y in range(Y)])


def per_device(pred_cov, cross, filt_mean, pred_mean, next_smoothed):
    steps = lax.axis_size("tm")
    row = lax.axis_index("row")
    y, z = row % Y, row // Y
    columns = jnp.stack([filt_mean[0], pred_mean[0], next_smoothed], axis=1)
    packed = jnp.concatenate([cross[0], jnp.pad(columns, ((0, 0), (0, LANES - 3)))], axis=1)
    first = (row * MINE).astype(jnp.uint32)
    mine = (steps - 1 - lax.axis_index("tm")).astype(jnp.int32)[None]
    pred_cov, first, mine = lax.optimization_barrier((pred_cov, first, mine))

    own = jnp.concatenate([pred_cov[0]] + [along_y(pred_cov[0], d) for d in range(1, Y)], axis=0)
    a1, b1 = swap(own, True), swap(own, False)
    packed, a1, b1 = lax.optimization_barrier((packed, a1, b1))
    packed = lax.all_gather(packed, "row", axis=0, tiled=True)
    a2, b2 = swap(b1, True), swap(a1, False)
    a3, b3 = swap(b2, True), swap(a2, False)
    b4 = swap(a3, False)
    e = 1 - 2 * (z % 2)
    at = lambda k: (z + e * k + Z) % Z
    order = [at(0) // 2, at(-1) // 2, at(2) // 2, at(-3) // 2]
    ids = lambda m, n: jnp.stack(order + [at(m), at(n), y, y]).astype(jnp.int32)
    w = sweep_stage(0, ids(0, 1), own, a1, None, None)[0]
    w = sweep_stage(1, ids(-1, -2), b1, b2, w, None)[0]
    w = sweep_stage(2, ids(2, 3), a2, a3, w, None)[0]
    minus_inverse, gain = sweep_stage(3, ids(-3, -4), b3, b4, w, cross[0])

    state, base, mean = turn(0, mine, minus_inverse, packed)
    for n in range(1, steps):
        late = lax.ppermute(state, "tm", [(steps - n, steps - n - 1)])
        (state,) = turn(n, mine, late, state, base, mean, minus_inverse, packed)
    smoothed = lax.dynamic_slice(state[0], (first,), (MINE,))
    return (smoothed[None, :], gain[None, :, :])


def solution(mesh):
    in_specs = (
        P("tm", "row", None),
        P("tm", "row", None),
        P("tm", "row"),
        P("tm", "row"),
        P("row"),
    )
    out_specs = (P("tm", "row"), P("tm", "row", None))
    return jax.shard_map(
        per_device, mesh=mesh, in_specs=in_specs, out_specs=out_specs, check_vma=False
    )
```

```python
import functools

import jax
import jax.numpy as jnp
from jax import lax
from jax.experimental import pallas as pl
from jax.experimental.pallas import tpu as pltpu
from jax.sharding import PartitionSpec as P

f32, bf16 = jnp.float32, jnp.bfloat16
N, LANES = 1536, 128
MINE = 48
PIECE = 4 * MINE
B = 2 * PIECE
H = 128
TILE = 512
Y, Z = 4, 8
VMEM_WHOLE = pl.BlockSpec(memory_space=pltpu.VMEM)
SMEM_WHOLE = pl.BlockSpec(memory_space=pltpu.SMEM)

def inv4(d):
    a,b,c=d[0][0],d[1][0],d[1][1]
    r=1.0/(a*c-b*b)
    p,q,s=c*r,-b*r,a*r
    e0,e1,g0,g1=d[2][0],d[2][1],d[3][0],d[3][1]
    x00,x01=e0*p+e1*q,e0*q+e1*s
    x10,x11=g0*p+g1*q,g0*q+g1*s
    u=d[2][2]-(x00*e0+x01*e1)
    v=d[3][2]-(x10*e0+x11*e1)
    w=d[3][3]-(x10*g0+x11*g1)
    r2=1.0/(u*w-v*v)
    U,V,W=w*r2,-v*r2,u*r2
    y00,y01=U*x00+V*x10,U*x01+V*x11
    y10,y11=V*x00+W*x10,V*x01+W*x11
    i00=p+x00*y00+x10*y10
    i01=q+x00*y01+x10*y11
    i11=s+x01*y01+x11*y11
    return [[i00,i01,-y00,-y10],[i01,i11,-y01,-y11],[-y00,-y01,U,V],[-y10,-y11,V,W]]

def leaf(m_ref, K=4):
    n=m_ref.shape[0]
    lane=lax.broadcasted_iota(jnp.int32,(1,n),1)
    lanef=lax.broadcasted_iota(jnp.int32,(n,n),1)
    for p0 in range(0,n,K):
        M=m_ref[...]
        c=[jnp.broadcast_to(M[:,p0+q:p0+q+1],(n,n)) for q in range(K)]
        d=[[c[j][p0+i:p0+i+1,:] for j in range(i+1)] for i in range(K)]
        Di=inv4(d)
        r=[M[p0+q:p0+q+1,:] for q in range(K)]
        t=[]
        for i in range(K):
            x=Di[i][0]*r[0]
            for j in range(1,K): x=x+Di[i][j]*r[j]
            for j in range(K): x=jnp.where(lane==p0+j,-Di[i][j],x)
            t.append(x)
        new=jnp.where((lanef>=p0)&(lanef<p0+K),0.0,M)
        for q in range(K): new=new-c[q]*t[q]
        m_ref[...]=new
        m_ref[p0:p0+K,:]=jnp.concatenate(t,0)


def split(x):
    h = x.astype(bf16)
    return h, (x - h.astype(f32)).astype(bf16)


def wide(x):
    h, l = split(x)
    return jnp.concatenate([h, h, l], 1)


def tall(x):
    h, l = split(x)
    return jnp.concatenate([h, l, h], 0)


def dot(a, b):
    return jnp.dot(a, b, preferred_element_type=f32)


def block_sweep(d_ref, m_ref, r_ref):
    def step(k, _):
        o = pl.multiple_of(k * H, H)
        m_ref[...] = d_ref[pl.ds(o, H), pl.ds(o, H)]
        leaf(m_ref)
        minus = m_ref[...]
        t = -dot(wide(minus), tall(d_ref[pl.ds(o, H), :]))
        c = wide(d_ref[:, pl.ds(o, H)])
        r_ref[...] = -dot(c, tall(minus))
        d_ref[...] = d_ref[...] - dot(c, tall(t))
        d_ref[pl.ds(o, H), :] = t
        d_ref[:, pl.ds(o, H)] = r_ref[...]
        d_ref[pl.ds(o, H), pl.ds(o, H)] = minus
        return 0

    lax.fori_loop(0, B // H, step, 0)


def stage_kernel(stage, ids, block_ref, *refs):
    if stage:
        _, *refs = refs
    w_ref, p_ref, t3_ref, d_ref, m_ref, r_ref = refs
    here = pl.multiple_of(ids[stage] * B, B)
    for n in range(2):
        for d in range(Y):
            y = lax.rem(ids[6] + d, Y)
            to = pl.multiple_of(lax.rem(ids[4 + n], 2) * PIECE + y * MINE, 16)
            at = (2 * d + n) * MINE
            p_ref[pl.ds(to, MINE), :] = block_ref[at : at + MINE, :]
    rows = pl.ds(here, B)
    w_ref[rows, :] = p_ref[...].astype(f32)
    if stage:

        def clear(j, _):
            w_ref[rows, pl.ds(pl.multiple_of(ids[j] * B, B), B)] = jnp.zeros((B, B), f32)
            return 0

        lax.fori_loop(0, stage, clear, 0)

        def earlier(j, _):
            there = pl.multiple_of(ids[j] * B, B)
            p = p_ref[:, pl.ds(there, B)]
            p = jnp.concatenate([p, p], 1)

            def tile(n, _):
                q = pl.ds(pl.multiple_of(n * TILE, TILE), TILE)
                h, l = split(w_ref[pl.ds(there, B), q])
                w_ref[rows, q] = w_ref[rows, q] - dot(p, jnp.concatenate([h, l], 0))
                return 0

            return lax.fori_loop(0, N // TILE, tile, 0)

        lax.fori_loop(0, stage, earlier, 0)
    d_ref[...] = w_ref[rows, pl.ds(here, B)]
    block_sweep(d_ref, m_ref, r_ref)
    minus = d_ref[...]
    left = wide(minus)

    def forward(n, _):
        q = pl.ds(pl.multiple_of(n * TILE, TILE), TILE)
        t = -dot(left, tall(w_ref[rows, q]))
        t3_ref[:, q] = tall(t)
        w_ref[rows, q] = t
        return 0

    lax.fori_loop(0, N // TILE, forward, 0)
    w_ref[rows, pl.ds(here, B)] = minus
    if stage:

        def update(j, _):
            back = pl.ds(pl.multiple_of(ids[j] * B, B), B)
            c = wide(w_ref[back, pl.ds(here, B)])
            d_ref[...] = -dot(c, tall(minus))

            def tile(n, _):
                q = pl.ds(pl.multiple_of(n * TILE, TILE), TILE)
                w_ref[back, q] = w_ref[back, q] - dot(c, t3_ref[:, q])
                return 0

            lax.fori_loop(0, N // TILE, tile, 0)
            w_ref[back, pl.ds(here, B)] = d_ref[...]
            return 0

        lax.fori_loop(0, stage, update, 0)


def gain_kernel(cross_ref, w_ref, g_ref):
    c3 = wide(cross_ref[...])

    def gains(j, _):
        q = pl.ds(pl.multiple_of(j * B, B), B)
        g_ref[:, q] = -dot(c3, tall(w_ref[:, q]))
        return 0

    lax.fori_loop(0, N // B, gains, 0)


def gain_rows(cross, minus_inverse):
    return pl.pallas_call(
        gain_kernel,
        name="gains",
        out_shape=jax.ShapeDtypeStruct(cross.shape, f32),
        in_specs=[VMEM_WHOLE] * 2,
        out_specs=VMEM_WHOLE,
        compiler_params=pltpu.CompilerParams(vmem_limit_bytes=12 << 20),
        cost_estimate=pl.CostEstimate(flops=1_000_000_000, bytes_accessed=4 * N * N, transcendentals=0),
    )(cross, minus_inverse)


def sweep_stage(stage, ids, block, w):
    args = [ids, block] + ([w] if stage else [])
    return pl.pallas_call(
        functools.partial(stage_kernel, stage),
        name="stage" + str(stage),
        out_shape=jax.ShapeDtypeStruct((N, N), f32),
        in_specs=[SMEM_WHOLE] + [VMEM_WHOLE] * (len(args) - 1),
        out_specs=VMEM_WHOLE,
        scratch_shapes=[
            pltpu.VMEM((B, N), bf16),
            pltpu.VMEM((3 * B, N), bf16),
            pltpu.VMEM((B, B), f32),
            pltpu.VMEM((H, H), f32),
            pltpu.VMEM((B, H), f32),
        ],
        input_output_aliases={2: 0} if stage else {},
        compiler_params=pltpu.CompilerParams(vmem_limit_bytes=STAGE_VMEM),
        cost_estimate=pl.CostEstimate(flops=40_000_000_000, bytes_accessed=4 * B * N, transcendentals=0),
    )(*args)


STAGE_VMEM = 24 << 20


def matvec(m_ref, v_ref, out_ref, part_ref):
    def block(i, _):
        rows = pl.ds(pl.multiple_of(i * LANES, LANES), LANES)
        total = m_ref[rows, :LANES] * v_ref[:, :LANES]
        for j in range(1, N // LANES):
            lanes = slice(j * LANES, (j + 1) * LANES)
            total = total + m_ref[rows, lanes] * v_ref[:, lanes]
        part_ref[rows, :] = total
        return 0

    lax.fori_loop(0, N // LANES, block, 0)
    for i in range(N // LANES):
        rows = slice(i * LANES, (i + 1) * LANES)
        out_ref[:, rows] = jnp.sum(part_ref[rows, :].T, axis=0, keepdims=True)


def turn_kernel(n, mine_ref, *refs):
    if n:
        late_ref, before_ref, base_ref, mean_ref, w_ref, x_ref, s_ref, v_ref, y_ref, part_ref = refs
    else:
        w_ref, x_ref, s_ref, base_ref, mean_ref, v_ref, y_ref, part_ref = refs
        for j in range(N // LANES):
            rows = slice(j * LANES, (j + 1) * LANES)
            vectors = x_ref[rows, N:].T[:8, :]
            mean_ref[:, rows] = vectors[0:1]
            base_ref[:, rows] = jnp.where(mine_ref[0] == 0, vectors[2:3], 0.0) - vectors[1:2]

    @pl.when(mine_ref[0] == n)
    def _():
        v_ref[...] = late_ref[...] + base_ref[...] if n else base_ref[...]
        matvec(w_ref, v_ref, y_ref, part_ref)
        matvec(x_ref, y_ref, s_ref, part_ref)
        s_ref[...] = mean_ref[...] - s_ref[...]

    @pl.when(mine_ref[0] != n)
    def _():
        s_ref[...] = before_ref[...] if n else mean_ref[...]


def turn(n, mine, *args):
    return pl.pallas_call(
        functools.partial(turn_kernel, n),
        name="turn" + str(n),
        out_shape=[jax.ShapeDtypeStruct((1, N), f32)] * (1 if n else 3),
        in_specs=[SMEM_WHOLE] + [VMEM_WHOLE] * len(args),
        out_specs=[VMEM_WHOLE] * (1 if n else 3),
        scratch_shapes=[pltpu.VMEM((1, N), f32), pltpu.VMEM((1, N), f32), pltpu.VMEM((N, LANES), f32)],
        compiler_params=pltpu.CompilerParams(vmem_limit_bytes=4 << 20),
        cost_estimate=pl.CostEstimate(flops=4 * N * N, bytes_accessed=8 * N * N, transcendentals=0),
    )(mine, *args)


def swap(x, inner):
    pairs = []
    for z in range(Z):
        other = z ^ 1 if inner else (z + (1 if z % 2 else -1)) % Z
        pairs += [(z * Y + y, other * Y + y) for y in range(Y)]
    return lax.ppermute(x, "row", pairs)


def along_y(x, d):
    return lax.ppermute(x, "row", [(z * Y + (y + d) % Y, z * Y + y) for z in range(Z) for y in range(Y)])


def per_device(pred_cov, cross, filt_mean, pred_mean, next_smoothed):
    steps = lax.axis_size("tm")
    row = lax.axis_index("row")
    y, z = row % Y, row // Y
    columns = jnp.stack([filt_mean[0], pred_mean[0], next_smoothed], axis=1)
    packed = jnp.concatenate([cross[0], jnp.pad(columns, ((0, 0), (0, LANES - 3)))], axis=1)
    first = (row * MINE).astype(jnp.uint32)
    mine = (steps - 1 - lax.axis_index("tm")).astype(jnp.int32)[None]
    pred_cov, first, mine = lax.optimization_barrier((pred_cov, first, mine))

    pair = jnp.concatenate([pred_cov[0], swap(pred_cov[0], True)], axis=0)
    pairs = [pair] + [along_y(pair, d) for d in range(1, Y)]
    own = jnp.concatenate(pairs, axis=0)
    packed, own = lax.optimization_barrier((packed, own))
    packed = lax.all_gather(packed, "row", axis=0, tiled=True)
    block1 = swap(own, False)
    block2 = swap(block1, True)
    block3 = swap(block2, False)
    e = 1 - 2 * (z % 2)
    at = lambda k: (z + e * k + Z) % Z
    order = [at(0) // 2, at(-1) // 2, at(2) // 2, at(-3) // 2]
    ids = lambda m, n: jnp.stack(order + [at(m), at(n), y, y]).astype(jnp.int32)
    w = sweep_stage(0, ids(0, 1), own, None)
    w = sweep_stage(1, ids(-1, -2), block1, w)
    w = sweep_stage(2, ids(2, 3), block2, w)
    w = sweep_stage(3, ids(-3, -4), block3, w)

    state, base, mean = turn(0, mine, w, packed)
    for n in range(1, steps):
        late = lax.ppermute(state, "tm", [(steps - n, steps - n - 1)])
        if n == steps // 2:
            gain = gain_rows(cross[0], w)
            late, gain = lax.optimization_barrier((late, gain))
        (state,) = turn(n, mine, late, state, base, mean, w, packed)
    smoothed = lax.dynamic_slice(state[0], (first,), (MINE,))
    return (smoothed[None, :], gain[None, :, :])


def solution(mesh):
    in_specs = (
        P("tm", "row", None),
        P("tm", "row", None),
        P("tm", "row"),
        P("tm", "row"),
        P("row"),
    )
    out_specs = (P("tm", "row"), P("tm", "row", None))
    return jax.shard_map(
        per_device, mesh=mesh, in_specs=in_specs, out_specs=out_specs, check_vma=False
    )
```

```python
import functools

import jax
import jax.numpy as jnp
from jax import lax
from jax.experimental import pallas as pl
from jax.experimental.pallas import tpu as pltpu
from jax.sharding import PartitionSpec as P

f32, bf16 = jnp.float32, jnp.bfloat16
N, LANES = 1536, 128
MINE = 48
PIECE = 4 * MINE
B = 2 * PIECE
H = 128
TILE = 512
Y, Z = 4, 8
VMEM_WHOLE = pl.BlockSpec(memory_space=pltpu.VMEM)
SMEM_WHOLE = pl.BlockSpec(memory_space=pltpu.SMEM)

def inv4(d):
    a,b,c=d[0][0],d[1][0],d[1][1]
    r=1.0/(a*c-b*b)
    p,q,s=c*r,-b*r,a*r
    e0,e1,g0,g1=d[2][0],d[2][1],d[3][0],d[3][1]
    x00,x01=e0*p+e1*q,e0*q+e1*s
    x10,x11=g0*p+g1*q,g0*q+g1*s
    u=d[2][2]-(x00*e0+x01*e1)
    v=d[3][2]-(x10*e0+x11*e1)
    w=d[3][3]-(x10*g0+x11*g1)
    r2=1.0/(u*w-v*v)
    U,V,W=w*r2,-v*r2,u*r2
    y00,y01=U*x00+V*x10,U*x01+V*x11
    y10,y11=V*x00+W*x10,V*x01+W*x11
    i00=p+x00*y00+x10*y10
    i01=q+x00*y01+x10*y11
    i11=s+x01*y01+x11*y11
    return [[i00,i01,-y00,-y10],[i01,i11,-y01,-y11],[-y00,-y01,U,V],[-y10,-y11,V,W]]

def leaf(m_ref, K=4):
    n=m_ref.shape[0]
    lane=lax.broadcasted_iota(jnp.int32,(1,n),1)
    lanef=lax.broadcasted_iota(jnp.int32,(n,n),1)
    for p0 in range(0,n,K):
        M=m_ref[...]
        c=[jnp.broadcast_to(M[:,p0+q:p0+q+1],(n,n)) for q in range(K)]
        d=[[c[j][p0+i:p0+i+1,:] for j in range(i+1)] for i in range(K)]
        Di=inv4(d)
        r=[M[p0+q:p0+q+1,:] for q in range(K)]
        t=[]
        for i in range(K):
            x=Di[i][0]*r[0]
            for j in range(1,K): x=x+Di[i][j]*r[j]
            for j in range(K): x=jnp.where(lane==p0+j,-Di[i][j],x)
            t.append(x)
        new=jnp.where((lanef>=p0)&(lanef<p0+K),0.0,M)
        for q in range(K): new=new-c[q]*t[q]
        m_ref[...]=new
        m_ref[p0:p0+K,:]=jnp.concatenate(t,0)


def split(x):
    h = x.astype(bf16)
    return h, (x - h.astype(f32)).astype(bf16)


def wide(x):
    h, l = split(x)
    return jnp.concatenate([h, h, l], 1)


def tall(x):
    h, l = split(x)
    return jnp.concatenate([h, l, h], 0)


def dot(a, b):
    return jnp.dot(a, b, preferred_element_type=f32)


def block_sweep(d_ref, m_ref, r_ref, odd=0, first_ref=None):
    def step(k, _):
        o = pl.multiple_of(jnp.where(odd > 0, B // H - 1 - k, k) * H, H)

        def sweep_leaf():
            m_ref[...] = d_ref[pl.ds(o, H), pl.ds(o, H)]
            leaf(m_ref)

        if first_ref is None:
            sweep_leaf()
        else:
            pl.when(k > 0)(sweep_leaf)

            @pl.when(k == 0)
            def _():
                m_ref[...] = first_ref[...]

        minus = m_ref[...]
        t = -dot(wide(minus), tall(d_ref[pl.ds(o, H), :]))
        c = wide(d_ref[:, pl.ds(o, H)])
        r_ref[...] = -dot(c, tall(minus))
        d_ref[...] = d_ref[...] - dot(c, tall(t))
        d_ref[pl.ds(o, H), :] = t
        d_ref[:, pl.ds(o, H)] = r_ref[...]
        d_ref[pl.ds(o, H), pl.ds(o, H)] = minus
        return 0

    lax.fori_loop(0, B // H, step, 0)


def stage_kernel(stage, ids, near_ref, far_ref, *refs):
    first_ref, *refs = refs
    w_ref, p_ref, t3_ref, d_ref, m_ref, r_ref = refs
    here = pl.multiple_of(ids[stage] * B, B)
    for n, ref in enumerate((near_ref, far_ref)):
        z = ids[4 + n]
        for d in range(Y):
            y = lax.rem(ids[6] + d, Y)
            to = pl.multiple_of(lax.rem(z, 2) * PIECE + y * MINE, 16)
            p_ref[pl.ds(to, MINE), :] = ref[d * MINE : (d + 1) * MINE, :]
    rows = pl.ds(here, B)
    w_ref[rows, :] = p_ref[...].astype(f32)
    if stage:

        def clear(j, _):
            w_ref[rows, pl.ds(pl.multiple_of(ids[j] * B, B), B)] = jnp.zeros((B, B), f32)
            return 0

        lax.fori_loop(0, stage, clear, 0)

        def earlier(j, _):
            there = pl.multiple_of(ids[j] * B, B)
            p = p_ref[:, pl.ds(there, B)]
            p = jnp.concatenate([p, p], 1)

            def tile(n, _):
                q = pl.ds(pl.multiple_of(n * TILE, TILE), TILE)
                h, l = split(w_ref[pl.ds(there, B), q])
                w_ref[rows, q] = w_ref[rows, q] - dot(p, jnp.concatenate([h, l], 0))
                return 0

            return lax.fori_loop(0, N // TILE, tile, 0)

        lax.fori_loop(0, stage, earlier, 0)
    d_ref[...] = w_ref[rows, pl.ds(here, B)]
    if stage:
        block_sweep(d_ref, m_ref, r_ref)
    else:
        block_sweep(d_ref, m_ref, r_ref, ids[7], first_ref)
    minus = d_ref[...]
    left = wide(minus)

    def forward(n, _):
        q = pl.ds(pl.multiple_of(n * TILE, TILE), TILE)
        t = -dot(left, tall(w_ref[rows, q]))
        t3_ref[:, q] = tall(t)
        w_ref[rows, q] = t
        return 0

    lax.fori_loop(0, N // TILE, forward, 0)
    w_ref[rows, pl.ds(here, B)] = minus
    if stage:

        def update(j, _):
            back = pl.ds(pl.multiple_of(ids[j] * B, B), B)
            c = wide(w_ref[back, pl.ds(here, B)])
            d_ref[...] = -dot(c, tall(minus))

            def tile(n, _):
                q = pl.ds(pl.multiple_of(n * TILE, TILE), TILE)
                w_ref[back, q] = w_ref[back, q] - dot(c, t3_ref[:, q])
                return 0

            lax.fori_loop(0, N // TILE, tile, 0)
            w_ref[back, pl.ds(here, B)] = d_ref[...]
            return 0

        lax.fori_loop(0, stage, update, 0)


def gain_kernel(cross_ref, w_ref, g_ref):
    c3 = wide(cross_ref[...])

    def gains(j, _):
        q = pl.ds(pl.multiple_of(j * B, B), B)
        g_ref[:, q] = -dot(c3, tall(w_ref[:, q]))
        return 0

    lax.fori_loop(0, N // B, gains, 0)


def gain_rows(cross, minus_inverse):
    return pl.pallas_call(
        gain_kernel,
        name="gains",
        out_shape=jax.ShapeDtypeStruct(cross.shape, f32),
        in_specs=[VMEM_WHOLE] * 2,
        out_specs=VMEM_WHOLE,
        compiler_params=pltpu.CompilerParams(vmem_limit_bytes=12 << 20),
        cost_estimate=pl.CostEstimate(flops=1_000_000_000, bytes_accessed=4 * N * N, transcendentals=0),
    )(cross, minus_inverse)


def first_leaf_kernel(ids, own_ref, m_ref, n_ref):
    odd = ids[7]
    lanes = pl.ds(pl.multiple_of(ids[0] * B + odd * (B - H), H), H)
    for d in range(Y):
        to = pl.multiple_of(lax.rem(ids[6] + d, Y) * MINE, 16)
        n_ref[pl.ds(to, MINE), :] = own_ref[d * MINE : (d + 1) * MINE, lanes]
    m_ref[...] = n_ref[pl.ds(pl.multiple_of(odd * (PIECE - H), 16), H), :].astype(f32)
    leaf(m_ref)


def first_leaf(ids, own):
    return pl.pallas_call(
        first_leaf_kernel,
        name="first_leaf",
        out_shape=jax.ShapeDtypeStruct((H, H), f32),
        in_specs=[SMEM_WHOLE, VMEM_WHOLE],
        out_specs=VMEM_WHOLE,
        scratch_shapes=[pltpu.VMEM((PIECE, H), bf16)],
        compiler_params=pltpu.CompilerParams(vmem_limit_bytes=4 << 20),
        cost_estimate=pl.CostEstimate(flops=6_000_000_000, bytes_accessed=2 * PIECE * N, transcendentals=0),
    )(ids, own)


def sweep_stage(stage, ids, near, far, other):
    return pl.pallas_call(
        functools.partial(stage_kernel, stage),
        name="stage" + str(stage),
        out_shape=jax.ShapeDtypeStruct((N, N), f32),
        in_specs=[SMEM_WHOLE] + [VMEM_WHOLE] * 3,
        out_specs=VMEM_WHOLE,
        scratch_shapes=[
            pltpu.VMEM((B, N), bf16),
            pltpu.VMEM((3 * B, N), bf16),
            pltpu.VMEM((B, B), f32),
            pltpu.VMEM((H, H), f32),
            pltpu.VMEM((B, H), f32),
        ],
        input_output_aliases={3: 0} if stage else {},
        compiler_params=pltpu.CompilerParams(vmem_limit_bytes=STAGE_VMEM),
        cost_estimate=pl.CostEstimate(flops=40_000_000_000, bytes_accessed=4 * B * N, transcendentals=0),
    )(ids, near, far, other)


STAGE_VMEM = 24 << 20


def matvec(m_ref, v_ref, out_ref, part_ref):
    def block(i, _):
        rows = pl.ds(pl.multiple_of(i * LANES, LANES), LANES)
        total = m_ref[rows, :LANES] * v_ref[:, :LANES]
        for j in range(1, N // LANES):
            lanes = slice(j * LANES, (j + 1) * LANES)
            total = total + m_ref[rows, lanes] * v_ref[:, lanes]
        part_ref[rows, :] = total
        return 0

    lax.fori_loop(0, N // LANES, block, 0)
    for i in range(N // LANES):
        rows = slice(i * LANES, (i + 1) * LANES)
        out_ref[:, rows] = jnp.sum(part_ref[rows, :].T, axis=0, keepdims=True)


def turn_kernel(n, mine_ref, *refs):
    if n:
        late_ref, before_ref, base_ref, mean_ref, w_ref, x_ref, s_ref, v_ref, y_ref, part_ref = refs
    else:
        w_ref, x_ref, s_ref, base_ref, mean_ref, v_ref, y_ref, part_ref = refs
        for j in range(N // LANES):
            rows = slice(j * LANES, (j + 1) * LANES)
            vectors = x_ref[rows, N:].T[:8, :]
            mean_ref[:, rows] = vectors[0:1]
            base_ref[:, rows] = jnp.where(mine_ref[0] == 0, vectors[2:3], 0.0) - vectors[1:2]

    @pl.when(mine_ref[0] == n)
    def _():
        v_ref[...] = late_ref[...] + base_ref[...] if n else base_ref[...]
        matvec(w_ref, v_ref, y_ref, part_ref)
        matvec(x_ref, y_ref, s_ref, part_ref)
        s_ref[...] = mean_ref[...] - s_ref[...]

    @pl.when(mine_ref[0] != n)
    def _():
        s_ref[...] = before_ref[...] if n else mean_ref[...]


def turn(n, mine, *args):
    return pl.pallas_call(
        functools.partial(turn_kernel, n),
        name="turn" + str(n),
        out_shape=[jax.ShapeDtypeStruct((1, N), f32)] * (1 if n else 3),
        in_specs=[SMEM_WHOLE] + [VMEM_WHOLE] * len(args),
        out_specs=[VMEM_WHOLE] * (1 if n else 3),
        scratch_shapes=[pltpu.VMEM((1, N), f32), pltpu.VMEM((1, N), f32), pltpu.VMEM((N, LANES), f32)],
        compiler_params=pltpu.CompilerParams(vmem_limit_bytes=4 << 20),
        cost_estimate=pl.CostEstimate(flops=4 * N * N, bytes_accessed=8 * N * N, transcendentals=0),
    )(mine, *args)


def swap(x, inner):
    pairs = []
    for z in range(Z):
        other = z ^ 1 if inner else (z + (1 if z % 2 else -1)) % Z
        pairs += [(z * Y + y, other * Y + y) for y in range(Y)]
    return lax.ppermute(x, "row", pairs)


def along_y(x, d):
    return lax.ppermute(x, "row", [(z * Y + (y + d) % Y, z * Y + y) for z in range(Z) for y in range(Y)])


def per_device(pred_cov, cross, filt_mean, pred_mean, next_smoothed):
    steps = lax.axis_size("tm")
    row = lax.axis_index("row")
    y, z = row % Y, row // Y
    columns = jnp.stack([filt_mean[0], pred_mean[0], next_smoothed], axis=1)
    packed = jnp.concatenate([cross[0], jnp.pad(columns, ((0, 0), (0, LANES - 3)))], axis=1)
    first = (row * MINE).astype(jnp.uint32)
    mine = (steps - 1 - lax.axis_index("tm")).astype(jnp.int32)[None]
    pred_cov, first, mine = lax.optimization_barrier((pred_cov, first, mine))

    own = jnp.concatenate([pred_cov[0]] + [along_y(pred_cov[0], d) for d in range(1, Y)], axis=0)
    packed, own = lax.optimization_barrier((packed, own))
    packed = lax.all_gather(packed, "row", axis=0, tiled=True)
    a1, b1 = swap(own, True), swap(own, False)
    a2, b2 = swap(b1, True), swap(a1, False)
    a3, b3 = swap(b2, True), swap(a2, False)
    b4 = swap(a3, False)
    e = 1 - 2 * (z % 2)
    at = lambda k: (z + e * k + Z) % Z
    order = [at(0) // 2, at(-1) // 2, at(2) // 2, at(-3) // 2]
    ids = lambda m, n: jnp.stack(order + [at(m), at(n), y, z % 2]).astype(jnp.int32)
    w = sweep_stage(0, ids(0, 1), own, a1, first_leaf(ids(0, 1), own))
    w = sweep_stage(1, ids(-1, -2), b1, b2, w)
    w = sweep_stage(2, ids(2, 3), a2, a3, w)
    w = sweep_stage(3, ids(-3, -4), b3, b4, w)

    state, base, mean = turn(0, mine, w, packed)
    for n in range(1, steps):
        late = lax.ppermute(state, "tm", [(steps - n, steps - n - 1)])
        if n == steps // 2:
            gain = gain_rows(cross[0], w)
            late, gain = lax.optimization_barrier((late, gain))
        (state,) = turn(n, mine, late, state, base, mean, w, packed)
    smoothed = lax.dynamic_slice(state[0], (first,), (MINE,))
    return (smoothed[None, :], gain[None, :, :])


def solution(mesh):
    in_specs = (
        P("tm", "row", None),
        P("tm", "row", None),
        P("tm", "row"),
        P("tm", "row"),
        P("row"),
    )
    out_specs = (P("tm", "row"), P("tm", "row", None))
    return jax.shard_map(
        per_device, mesh=mesh, in_specs=in_specs, out_specs=out_specs, check_vma=False
    )
```

```python
import functools

import jax
import jax.numpy as jnp
from jax import lax
from jax.experimental import pallas as pl
from jax.experimental.pallas import tpu as pltpu
from jax.sharding import PartitionSpec as P

f32, bf16 = jnp.float32, jnp.bfloat16
N, LANES = 1536, 128
MINE = 48
PIECE = 4 * MINE
B = 2 * PIECE
H = 128
TILE = 512
Y, Z = 4, 8
VMEM_WHOLE = pl.BlockSpec(memory_space=pltpu.VMEM)
SMEM_WHOLE = pl.BlockSpec(memory_space=pltpu.SMEM)

def inv4(d):
    a,b,c=d[0][0],d[1][0],d[1][1]
    r=1.0/(a*c-b*b)
    p,q,s=c*r,-b*r,a*r
    e0,e1,g0,g1=d[2][0],d[2][1],d[3][0],d[3][1]
    x00,x01=e0*p+e1*q,e0*q+e1*s
    x10,x11=g0*p+g1*q,g0*q+g1*s
    u=d[2][2]-(x00*e0+x01*e1)
    v=d[3][2]-(x10*e0+x11*e1)
    w=d[3][3]-(x10*g0+x11*g1)
    r2=1.0/(u*w-v*v)
    U,V,W=w*r2,-v*r2,u*r2
    y00,y01=U*x00+V*x10,U*x01+V*x11
    y10,y11=V*x00+W*x10,V*x01+W*x11
    i00=p+x00*y00+x10*y10
    i01=q+x00*y01+x10*y11
    i11=s+x01*y01+x11*y11
    return [[i00,i01,-y00,-y10],[i01,i11,-y01,-y11],[-y00,-y01,U,V],[-y10,-y11,V,W]]

def leaf(m_ref, K=4):
    n=m_ref.shape[0]
    lane=lax.broadcasted_iota(jnp.int32,(1,n),1)
    lanef=lax.broadcasted_iota(jnp.int32,(n,n),1)
    for p0 in range(0,n,K):
        M=m_ref[...]
        c=[jnp.broadcast_to(M[:,p0+q:p0+q+1],(n,n)) for q in range(K)]
        d=[[c[j][p0+i:p0+i+1,:] for j in range(i+1)] for i in range(K)]
        Di=inv4(d)
        r=[M[p0+q:p0+q+1,:] for q in range(K)]
        t=[]
        for i in range(K):
            x=Di[i][0]*r[0]
            for j in range(1,K): x=x+Di[i][j]*r[j]
            for j in range(K): x=jnp.where(lane==p0+j,-Di[i][j],x)
            t.append(x)
        new=jnp.where((lanef>=p0)&(lanef<p0+K),0.0,M)
        for q in range(K): new=new-c[q]*t[q]
        m_ref[...]=new
        m_ref[p0:p0+K,:]=jnp.concatenate(t,0)


def split(x):
    h = x.astype(bf16)
    return h, (x - h.astype(f32)).astype(bf16)


def wide(x):
    h, l = split(x)
    return jnp.concatenate([h, h, l], 1)


def tall(x):
    h, l = split(x)
    return jnp.concatenate([h, l, h], 0)


def dot(a, b):
    return jnp.dot(a, b, preferred_element_type=f32)


def block_sweep(d_ref, m_ref, r_ref):
    def step(k, _):
        o = pl.multiple_of(k * H, H)
        m_ref[...] = d_ref[pl.ds(o, H), pl.ds(o, H)]
        leaf(m_ref)
        minus = m_ref[...]
        t = -dot(wide(minus), tall(d_ref[pl.ds(o, H), :]))
        c = wide(d_ref[:, pl.ds(o, H)])
        r_ref[...] = -dot(c, tall(minus))
        d_ref[...] = d_ref[...] - dot(c, tall(t))
        d_ref[pl.ds(o, H), :] = t
        d_ref[:, pl.ds(o, H)] = r_ref[...]
        d_ref[pl.ds(o, H), pl.ds(o, H)] = minus
        return 0

    lax.fori_loop(0, B // H, step, 0)


def stage_kernel(stage, ids, *refs):
    before_ref, w_ref, p_ref, t3_ref, d_ref, m_ref, r_ref = refs[Y:]
    here = pl.multiple_of(ids[stage] * B, B)
    place(ids, refs[:Y], p_ref)
    rows = pl.ds(here, B)
    w_ref[rows, :] = p_ref[...].astype(f32)
    if stage:

        def clear(j, _):
            w_ref[rows, pl.ds(pl.multiple_of(ids[j] * B, B), B)] = jnp.zeros((B, B), f32)
            return 0

        lax.fori_loop(0, stage, clear, 0)

        def earlier(j, _):
            there = pl.multiple_of(ids[j] * B, B)
            p = p_ref[:, pl.ds(there, B)]
            p = jnp.concatenate([p, p], 1)

            def tile(n, _):
                q = pl.ds(pl.multiple_of(n * TILE, TILE), TILE)
                h, l = split(w_ref[pl.ds(there, B), q])
                w_ref[rows, q] = w_ref[rows, q] - dot(p, jnp.concatenate([h, l], 0))
                return 0

            return lax.fori_loop(0, N // TILE, tile, 0)

        lax.fori_loop(0, stage, earlier, 0)
    if stage:
        d_ref[...] = w_ref[rows, pl.ds(here, B)]
        block_sweep(d_ref, m_ref, r_ref)
    else:
        d_ref[...] = before_ref[...]
    minus = d_ref[...]
    left = wide(minus)

    def forward(n, _):
        q = pl.ds(pl.multiple_of(n * TILE, TILE), TILE)
        t = -dot(left, tall(w_ref[rows, q]))
        t3_ref[:, q] = tall(t)
        w_ref[rows, q] = t
        return 0

    lax.fori_loop(0, N // TILE, forward, 0)
    w_ref[rows, pl.ds(here, B)] = minus
    if stage:

        def update(j, _):
            back = pl.ds(pl.multiple_of(ids[j] * B, B), B)
            c = wide(w_ref[back, pl.ds(here, B)])
            d_ref[...] = -dot(c, tall(minus))

            def tile(n, _):
                q = pl.ds(pl.multiple_of(n * TILE, TILE), TILE)
                w_ref[back, q] = w_ref[back, q] - dot(c, t3_ref[:, q])
                return 0

            lax.fori_loop(0, N // TILE, tile, 0)
            w_ref[back, pl.ds(here, B)] = d_ref[...]
            return 0

        lax.fori_loop(0, stage, update, 0)


def gain_kernel(cross_ref, w_ref, g_ref):
    c3 = wide(cross_ref[...])

    def gains(j, _):
        q = pl.ds(pl.multiple_of(j * B, B), B)
        g_ref[:, q] = -dot(c3, tall(w_ref[:, q]))
        return 0

    lax.fori_loop(0, N // B, gains, 0)


def gain_rows(cross, minus_inverse):
    return pl.pallas_call(
        gain_kernel,
        name="gains",
        out_shape=jax.ShapeDtypeStruct(cross.shape, f32),
        in_specs=[VMEM_WHOLE] * 2,
        out_specs=VMEM_WHOLE,
        compiler_params=pltpu.CompilerParams(vmem_limit_bytes=12 << 20),
        cost_estimate=pl.CostEstimate(flops=1_000_000_000, bytes_accessed=4 * N * N, transcendentals=0),
    )(cross, minus_inverse)


def place(ids, refs, to_ref):
    for d, ref in enumerate(refs):
        for n in range(2):
            y = lax.rem(ids[6] + d, Y)
            to = pl.multiple_of(lax.rem(ids[4 + n], 2) * PIECE + y * MINE, 16)
            to_ref[pl.ds(to, MINE), :] = ref[n * MINE : (n + 1) * MINE, :].astype(to_ref.dtype)


def own_block_kernel(ids, *refs):
    d_ref, m_ref, r_ref = refs[Y:]
    place(ids, refs[:Y], d_ref)
    block_sweep(d_ref, m_ref, r_ref)


def own_block(ids, pieces):
    return pl.pallas_call(
        own_block_kernel,
        name="own_block",
        out_shape=jax.ShapeDtypeStruct((B, B), f32),
        in_specs=[SMEM_WHOLE] + [VMEM_WHOLE] * Y,
        out_specs=VMEM_WHOLE,
        scratch_shapes=[pltpu.VMEM((H, H), f32), pltpu.VMEM((B, H), f32)],
        compiler_params=pltpu.CompilerParams(vmem_limit_bytes=8 << 20),
        cost_estimate=pl.CostEstimate(flops=20_000_000_000, bytes_accessed=2 * B * B, transcendentals=0),
    )(ids, *pieces)


def sweep_stage(stage, ids, pieces, before):
    return pl.pallas_call(
        functools.partial(stage_kernel, stage),
        name="stage" + str(stage),
        out_shape=jax.ShapeDtypeStruct((N, N), f32),
        in_specs=[SMEM_WHOLE] + [VMEM_WHOLE] * (Y + 1),
        out_specs=VMEM_WHOLE,
        scratch_shapes=[
            pltpu.VMEM((B, N), bf16),
            pltpu.VMEM((3 * B, N), bf16),
            pltpu.VMEM((B, B), f32),
            pltpu.VMEM((H, H), f32),
            pltpu.VMEM((B, H), f32),
        ],
        input_output_aliases={Y + 1: 0} if stage else {},
        compiler_params=pltpu.CompilerParams(vmem_limit_bytes=STAGE_VMEM),
        cost_estimate=pl.CostEstimate(flops=40_000_000_000, bytes_accessed=4 * B * N, transcendentals=0),
    )(ids, *pieces, before)


STAGE_VMEM = 24 << 20


def matvec(m_ref, v_ref, out_ref, part_ref):
    def block(i, _):
        rows = pl.ds(pl.multiple_of(i * LANES, LANES), LANES)
        total = m_ref[rows, :LANES] * v_ref[:, :LANES]
        for j in range(1, N // LANES):
            lanes = slice(j * LANES, (j + 1) * LANES)
            total = total + m_ref[rows, lanes] * v_ref[:, lanes]
        part_ref[rows, :] = total
        return 0

    lax.fori_loop(0, N // LANES, block, 0)
    for i in range(N // LANES):
        rows = slice(i * LANES, (i + 1) * LANES)
        out_ref[:, rows] = jnp.sum(part_ref[rows, :].T, axis=0, keepdims=True)


def turn_kernel(n, mine_ref, *refs):
    if n:
        late_ref, before_ref, base_ref, mean_ref, w_ref, x_ref, s_ref, v_ref, y_ref, part_ref = refs
    else:
        w_ref, x_ref, s_ref, base_ref, mean_ref, v_ref, y_ref, part_ref = refs
        for j in range(N // LANES):
            rows = slice(j * LANES, (j + 1) * LANES)
            vectors = x_ref[rows, N:].T[:8, :]
            mean_ref[:, rows] = vectors[0:1]
            base_ref[:, rows] = jnp.where(mine_ref[0] == 0, vectors[2:3], 0.0) - vectors[1:2]

    @pl.when(mine_ref[0] == n)
    def _():
        v_ref[...] = late_ref[...] + base_ref[...] if n else base_ref[...]
        matvec(w_ref, v_ref, y_ref, part_ref)
        matvec(x_ref, y_ref, s_ref, part_ref)
        s_ref[...] = mean_ref[...] - s_ref[...]

    @pl.when(mine_ref[0] != n)
    def _():
        s_ref[...] = before_ref[...] if n else mean_ref[...]


def turn(n, mine, *args):
    return pl.pallas_call(
        functools.partial(turn_kernel, n),
        name="turn" + str(n),
        out_shape=[jax.ShapeDtypeStruct((1, N), f32)] * (1 if n else 3),
        in_specs=[SMEM_WHOLE] + [VMEM_WHOLE] * len(args),
        out_specs=[VMEM_WHOLE] * (1 if n else 3),
        scratch_shapes=[pltpu.VMEM((1, N), f32), pltpu.VMEM((1, N), f32), pltpu.VMEM((N, LANES), f32)],
        compiler_params=pltpu.CompilerParams(vmem_limit_bytes=4 << 20),
        cost_estimate=pl.CostEstimate(flops=4 * N * N, bytes_accessed=8 * N * N, transcendentals=0),
    )(mine, *args)


def swap(x, inner):
    pairs = []
    for z in range(Z):
        other = z ^ 1 if inner else (z + (1 if z % 2 else -1)) % Z
        pairs += [(z * Y + y, other * Y + y) for y in range(Y)]
    return lax.ppermute(x, "row", pairs)


def along_y(x, d):
    return lax.ppermute(x, "row", [(z * Y + (y + d) % Y, z * Y + y) for z in range(Z) for y in range(Y)])


def per_device(pred_cov, cross, filt_mean, pred_mean, next_smoothed):
    steps = lax.axis_size("tm")
    row = lax.axis_index("row")
    y, z = row % Y, row // Y
    columns = jnp.stack([filt_mean[0], pred_mean[0], next_smoothed], axis=1)
    packed = jnp.concatenate([cross[0], jnp.pad(columns, ((0, 0), (0, LANES - 3)))], axis=1)
    first = (row * MINE).astype(jnp.uint32)
    mine = (steps - 1 - lax.axis_index("tm")).astype(jnp.int32)[None]
    pred_cov, first, mine = lax.optimization_barrier((pred_cov, first, mine))

    def along_all_y(x):
        return [x] + [along_y(x, d) for d in range(1, Y)]

    def strips(x):
        return jnp.concatenate([x, swap(x, True)], axis=0)

    diagonal = lax.dynamic_slice(pred_cov[0], (jnp.uint32(0), (z // 2 * B).astype(jnp.uint32)), (MINE, B))
    diagonal, rest = lax.optimization_barrier((strips(diagonal), pred_cov[0]))
    diagonal = along_all_y(diagonal)
    strip0, packed = lax.optimization_barrier((strips(rest), packed))
    packed = lax.all_gather(packed, "row", axis=0, tiled=True)
    strip1 = swap(strip0, False)
    strip2 = swap(strip1, True)
    strip3 = swap(strip2, False)
    e = 1 - 2 * (z % 2)
    at = lambda k: (z + e * k + Z) % Z
    order = [at(0) // 2, at(-1) // 2, at(2) // 2, at(-3) // 2]
    ids = lambda m, n: jnp.stack(order + [at(m), at(n), y, y]).astype(jnp.int32)
    w = sweep_stage(0, ids(0, 1), along_all_y(strip0), own_block(ids(0, 1), diagonal))
    w = sweep_stage(1, ids(-1, -2), along_all_y(strip1), w)
    w = sweep_stage(2, ids(2, 3), along_all_y(strip2), w)
    w = sweep_stage(3, ids(-3, -4), along_all_y(strip3), w)

    state, base, mean = turn(0, mine, w, packed)
    for n in range(1, steps):
        late = lax.ppermute(state, "tm", [(steps - n, steps - n - 1)])
        if n == steps // 2:
            gain = gain_rows(cross[0], w)
            late, gain = lax.optimization_barrier((late, gain))
        (state,) = turn(n, mine, late, state, base, mean, w, packed)
    smoothed = lax.dynamic_slice(state[0], (first,), (MINE,))
    return (smoothed[None, :], gain[None, :, :])


def solution(mesh):
    in_specs = (
        P("tm", "row", None),
        P("tm", "row", None),
        P("tm", "row"),
        P("tm", "row"),
        P("row"),
    )
    out_specs = (P("tm", "row"), P("tm", "row", None))
    return jax.shard_map(
        per_device, mesh=mesh, in_specs=in_specs, out_specs=out_specs, check_vma=False
    )
```

```python
import functools

import jax
import jax.numpy as jnp
from jax import lax
from jax.experimental import pallas as pl
from jax.experimental.pallas import tpu as pltpu
from jax.sharding import PartitionSpec as P

f32, bf16 = jnp.float32, jnp.bfloat16
N, LANES = 1536, 128
MINE = 48
PIECE = 4 * MINE
B = 2 * PIECE
H = 128
TILE = 512
Y, Z = 4, 8
VMEM_WHOLE = pl.BlockSpec(memory_space=pltpu.VMEM)
SMEM_WHOLE = pl.BlockSpec(memory_space=pltpu.SMEM)

def inv4(d):
    a,b,c=d[0][0],d[1][0],d[1][1]
    r=1.0/(a*c-b*b)
    p,q,s=c*r,-b*r,a*r
    e0,e1,g0,g1=d[2][0],d[2][1],d[3][0],d[3][1]
    x00,x01=e0*p+e1*q,e0*q+e1*s
    x10,x11=g0*p+g1*q,g0*q+g1*s
    u=d[2][2]-(x00*e0+x01*e1)
    v=d[3][2]-(x10*e0+x11*e1)
    w=d[3][3]-(x10*g0+x11*g1)
    r2=1.0/(u*w-v*v)
    U,V,W=w*r2,-v*r2,u*r2
    y00,y01=U*x00+V*x10,U*x01+V*x11
    y10,y11=V*x00+W*x10,V*x01+W*x11
    i00=p+x00*y00+x10*y10
    i01=q+x00*y01+x10*y11
    i11=s+x01*y01+x11*y11
    return [[i00,i01,-y00,-y10],[i01,i11,-y01,-y11],[-y00,-y01,U,V],[-y10,-y11,V,W]]


def product(a, b):
    return [[sum(x[k] * b[k][j] for k in range(4)) for j in range(4)] for x in a]


def inv8(d):
    a = inv4(d[:4])
    e = [row[:4] for row in d[4:]]
    x = product(e, a)
    s = [[d[4 + i][4 + j] - sum(x[i][k] * e[j][k] for k in range(4)) for j in range(i + 1)] for i in range(4)]
    w = inv4(s)
    y = product(w, x)
    top = [[None] * 4 for _ in range(4)]
    for i in range(4):
        for j in range(i + 1):
            top[i][j] = top[j][i] = a[i][j] + sum(x[k][i] * y[k][j] for k in range(4))
    upper = [top[i] + [-y[k][i] for k in range(4)] for i in range(4)]
    return upper + [[-v for v in y[i]] + w[i] for i in range(4)]


def leaf(m_ref):
    k, rows = 8, H // 8
    full = lambda x: jnp.broadcast_to(x, (k, H))
    lane = lax.broadcasted_iota(jnp.int32, (k, H), 1)
    sub = lax.broadcasted_iota(jnp.int32, (k, H), 0)
    m = [m_ref[k * v : k * v + k, :] for v in range(rows)]
    for p in range(rows):
        o = p * k
        r = [full(m[p][i : i + 1, :]) for i in range(k)]
        d = [[full(r[i][:, o + j : o + j + 1]) for j in range(i + 1)] for i in range(k)]
        inverse = inv8(d)
        pivots = (lane >= o) & (lane < o + k)
        r = [jnp.where(lane == o + i, -1.0, jnp.where(pivots, 0.0, r[i])) for i in range(k)]
        t = [sum(inverse[i][j] * r[j] for j in range(k)) for i in range(k)]
        new = list(m)
        for v in [(p + 1 + n) % rows for n in range(rows - 1)]:
            x = jnp.where(pivots, 0.0, m[v])
            for q in range(k):
                x = x - full(m[v][:, o + q : o + q + 1]) * t[q]
            new[v] = x
        new[p] = t[0]
        for i in range(1, k):
            new[p] = jnp.where(sub == i, t[i], new[p])
        m = new
    for v in range(rows):
        m_ref[k * v : k * v + k, :] = m[v]


def split(x):
    h = x.astype(bf16)
    return h, (x - h.astype(f32)).astype(bf16)


def wide(x):
    h, l = split(x)
    return jnp.concatenate([h, h, l], 1)


def tall(x):
    h, l = split(x)
    return jnp.concatenate([h, l, h], 0)


def dot(a, b):
    return jnp.dot(a, b, preferred_element_type=f32)


def block_sweep(d_ref, m_ref, r_ref, odd=0, first_ref=None):
    def step(k, _):
        o = pl.multiple_of(jnp.where(odd > 0, B // H - 1 - k, k) * H, H)

        def sweep_leaf():
            m_ref[...] = d_ref[pl.ds(o, H), pl.ds(o, H)]
            leaf(m_ref)

        if first_ref is None:
            sweep_leaf()
        else:
            pl.when(k > 0)(sweep_leaf)

            @pl.when(k == 0)
            def _():
                m_ref[...] = first_ref[...]

        minus = m_ref[...]
        t = -dot(wide(minus), tall(d_ref[pl.ds(o, H), :]))
        c = wide(d_ref[:, pl.ds(o, H)])
        r_ref[...] = -dot(c, tall(minus))
        d_ref[...] = d_ref[...] - dot(c, tall(t))
        d_ref[pl.ds(o, H), :] = t
        d_ref[:, pl.ds(o, H)] = r_ref[...]
        d_ref[pl.ds(o, H), pl.ds(o, H)] = minus
        return 0

    lax.fori_loop(0, B // H, step, 0)


def stage_kernel(stage, ids, near_ref, far_ref, *refs):
    first_ref, *refs = refs
    w_ref, p_ref, t3_ref, d_ref, m_ref, r_ref = refs
    here = pl.multiple_of(ids[stage] * B, B)
    for n, ref in enumerate((near_ref, far_ref)):
        z = ids[4 + n]
        for d in range(Y):
            y = lax.rem(ids[6] + d, Y)
            to = pl.multiple_of(lax.rem(z, 2) * PIECE + y * MINE, 16)
            p_ref[pl.ds(to, MINE), :] = ref[d * MINE : (d + 1) * MINE, :]
    rows = pl.ds(here, B)
    w_ref[rows, :] = p_ref[...].astype(f32)
    if stage:

        def clear(j, _):
            w_ref[rows, pl.ds(pl.multiple_of(ids[j] * B, B), B)] = jnp.zeros((B, B), f32)
            return 0

        lax.fori_loop(0, stage, clear, 0)

        def earlier(j, _):
            there = pl.multiple_of(ids[j] * B, B)
            p = p_ref[:, pl.ds(there, B)]
            p = jnp.concatenate([p, p], 1)

            def tile(n, _):
                q = pl.ds(pl.multiple_of(n * TILE, TILE), TILE)
                h, l = split(w_ref[pl.ds(there, B), q])
                w_ref[rows, q] = w_ref[rows, q] - dot(p, jnp.concatenate([h, l], 0))
                return 0

            return lax.fori_loop(0, N // TILE, tile, 0)

        lax.fori_loop(0, stage, earlier, 0)
    d_ref[...] = w_ref[rows, pl.ds(here, B)]
    if stage:
        block_sweep(d_ref, m_ref, r_ref)
    else:
        block_sweep(d_ref, m_ref, r_ref, ids[7], first_ref)
    minus = d_ref[...]
    left = wide(minus)

    def forward(n, _):
        q = pl.ds(pl.multiple_of(n * TILE, TILE), TILE)
        t = -dot(left, tall(w_ref[rows, q]))
        t3_ref[:, q] = tall(t)
        w_ref[rows, q] = t
        return 0

    lax.fori_loop(0, N // TILE, forward, 0)
    w_ref[rows, pl.ds(here, B)] = minus
    if stage:

        def update(j, _):
            back = pl.ds(pl.multiple_of(ids[j] * B, B), B)
            c = wide(w_ref[back, pl.ds(here, B)])
            d_ref[...] = -dot(c, tall(minus))

            def tile(n, _):
                q = pl.ds(pl.multiple_of(n * TILE, TILE), TILE)
                w_ref[back, q] = w_ref[back, q] - dot(c, t3_ref[:, q])
                return 0

            lax.fori_loop(0, N // TILE, tile, 0)
            w_ref[back, pl.ds(here, B)] = d_ref[...]
            return 0

        lax.fori_loop(0, stage, update, 0)


def gain_kernel(cross_ref, w_ref, g_ref):
    c3 = wide(cross_ref[...])

    def gains(j, _):
        q = pl.ds(pl.multiple_of(j * B, B), B)
        g_ref[:, q] = -dot(c3, tall(w_ref[:, q]))
        return 0

    lax.fori_loop(0, N // B, gains, 0)


def gain_rows(cross, minus_inverse):
    return pl.pallas_call(
        gain_kernel,
        name="gains",
        out_shape=jax.ShapeDtypeStruct(cross.shape, f32),
        in_specs=[VMEM_WHOLE] * 2,
        out_specs=VMEM_WHOLE,
        compiler_params=pltpu.CompilerParams(vmem_limit_bytes=12 << 20),
        cost_estimate=pl.CostEstimate(flops=1_000_000_000, bytes_accessed=4 * N * N, transcendentals=0),
    )(cross, minus_inverse)


def first_leaf_kernel(ids, own_ref, m_ref, n_ref):
    odd = ids[7]
    lanes = pl.ds(pl.multiple_of(ids[0] * B + odd * (B - H), H), H)
    for d in range(Y):
        to = pl.multiple_of(lax.rem(ids[6] + d, Y) * MINE, 16)
        n_ref[pl.ds(to, MINE), :] = own_ref[d * MINE : (d + 1) * MINE, lanes]
    m_ref[...] = n_ref[pl.ds(pl.multiple_of(odd * (PIECE - H), 16), H), :].astype(f32)
    leaf(m_ref)


def first_leaf(ids, own):
    return pl.pallas_call(
        first_leaf_kernel,
        name="first_leaf",
        out_shape=jax.ShapeDtypeStruct((H, H), f32),
        in_specs=[SMEM_WHOLE, VMEM_WHOLE],
        out_specs=VMEM_WHOLE,
        scratch_shapes=[pltpu.VMEM((PIECE, H), bf16)],
        compiler_params=pltpu.CompilerParams(vmem_limit_bytes=4 << 20),
        cost_estimate=pl.CostEstimate(flops=6_000_000_000, bytes_accessed=2 * PIECE * N, transcendentals=0),
    )(ids, own)


def sweep_stage(stage, ids, near, far, other):
    return pl.pallas_call(
        functools.partial(stage_kernel, stage),
        name="stage" + str(stage),
        out_shape=jax.ShapeDtypeStruct((N, N), f32),
        in_specs=[SMEM_WHOLE] + [VMEM_WHOLE] * 3,
        out_specs=VMEM_WHOLE,
        scratch_shapes=[
            pltpu.VMEM((B, N), bf16),
            pltpu.VMEM((3 * B, N), bf16),
            pltpu.VMEM((B, B), f32),
            pltpu.VMEM((H, H), f32),
            pltpu.VMEM((B, H), f32),
        ],
        input_output_aliases={3: 0} if stage else {},
        compiler_params=pltpu.CompilerParams(vmem_limit_bytes=STAGE_VMEM),
        cost_estimate=pl.CostEstimate(flops=40_000_000_000, bytes_accessed=4 * B * N, transcendentals=0),
    )(ids, near, far, other)


STAGE_VMEM = 24 << 20


def matvec(m_ref, v_ref, out_ref, part_ref):
    def block(i, _):
        rows = pl.ds(pl.multiple_of(i * LANES, LANES), LANES)
        total = m_ref[rows, :LANES] * v_ref[:, :LANES]
        for j in range(1, N // LANES):
            lanes = slice(j * LANES, (j + 1) * LANES)
            total = total + m_ref[rows, lanes] * v_ref[:, lanes]
        part_ref[rows, :] = total
        return 0

    lax.fori_loop(0, N // LANES, block, 0, unroll=4)
    for i in range(N // LANES):
        rows = slice(i * LANES, (i + 1) * LANES)
        out_ref[:, rows] = jnp.sum(part_ref[rows, :].T, axis=0, keepdims=True)


def turn_kernel(n, mine_ref, *refs):
    if n:
        late_ref, before_ref, base_ref, mean_ref, w_ref, x_ref, s_ref, v_ref, y_ref, part_ref = refs
    else:
        w_ref, x_ref, s_ref, base_ref, mean_ref, v_ref, y_ref, part_ref = refs
        for j in range(N // LANES):
            rows = slice(j * LANES, (j + 1) * LANES)
            vectors = x_ref[rows, N:].T[:8, :]
            mean_ref[:, rows] = vectors[0:1]
            base_ref[:, rows] = jnp.where(mine_ref[0] == 0, vectors[2:3], 0.0) - vectors[1:2]

    @pl.when(mine_ref[0] == n)
    def _():
        v_ref[...] = late_ref[...] + base_ref[...] if n else base_ref[...]
        matvec(w_ref, v_ref, y_ref, part_ref)
        matvec(x_ref, y_ref, s_ref, part_ref)
        s_ref[...] = mean_ref[...] - s_ref[...]

    @pl.when(mine_ref[0] != n)
    def _():
        s_ref[...] = before_ref[...] if n else mean_ref[...]


def turn(n, mine, *args):
    return pl.pallas_call(
        functools.partial(turn_kernel, n),
        name="turn" + str(n),
        out_shape=[jax.ShapeDtypeStruct((1, N), f32)] * (1 if n else 3),
        in_specs=[SMEM_WHOLE] + [VMEM_WHOLE] * len(args),
        out_specs=[VMEM_WHOLE] * (1 if n else 3),
        scratch_shapes=[pltpu.VMEM((1, N), f32), pltpu.VMEM((1, N), f32), pltpu.VMEM((N, LANES), f32)],
        compiler_params=pltpu.CompilerParams(vmem_limit_bytes=4 << 20),
        cost_estimate=pl.CostEstimate(flops=4 * N * N, bytes_accessed=8 * N * N, transcendentals=0),
    )(mine, *args)


def swap(x, inner):
    pairs = []
    for z in range(Z):
        other = z ^ 1 if inner else (z + (1 if z % 2 else -1)) % Z
        pairs += [(z * Y + y, other * Y + y) for y in range(Y)]
    return lax.ppermute(x, "row", pairs)


def along_y(x, d):
    return lax.ppermute(x, "row", [(z * Y + (y + d) % Y, z * Y + y) for z in range(Z) for y in range(Y)])


def per_device(pred_cov, cross, filt_mean, pred_mean, next_smoothed):
    steps = lax.axis_size("tm")
    row = lax.axis_index("row")
    y, z = row % Y, row // Y
    columns = jnp.stack([filt_mean[0], pred_mean[0], next_smoothed], axis=1)
    packed = jnp.concatenate([cross[0], jnp.pad(columns, ((0, 0), (0, LANES - 3)))], axis=1)
    first = (row * MINE).astype(jnp.uint32)
    mine = (steps - 1 - lax.axis_index("tm")).astype(jnp.int32)[None]
    pred_cov, first, mine = lax.optimization_barrier((pred_cov, first, mine))

    own = jnp.concatenate([pred_cov[0]] + [along_y(pred_cov[0], d) for d in range(1, Y)], axis=0)
    packed, own = lax.optimization_barrier((packed, own))
    packed = lax.all_gather(packed, "row", axis=0, tiled=True)
    a1, b1 = swap(own, True), swap(own, False)
    a2, b2 = swap(b1, True), swap(a1, False)
    a3, b3 = swap(b2, True), swap(a2, False)
    b4 = swap(a3, False)
    e = 1 - 2 * (z % 2)
    at = lambda k: (z + e * k + Z) % Z
    order = [at(0) // 2, at(-1) // 2, at(2) // 2, at(-3) // 2]
    ids = lambda m, n: jnp.stack(order + [at(m), at(n), y, z % 2]).astype(jnp.int32)
    w = sweep_stage(0, ids(0, 1), own, a1, first_leaf(ids(0, 1), own))
    w = sweep_stage(1, ids(-1, -2), b1, b2, w)
    w = sweep_stage(2, ids(2, 3), a2, a3, w)
    w = sweep_stage(3, ids(-3, -4), b3, b4, w)

    state, base, mean = turn(0, mine, w, packed)
    for n in range(1, steps):
        late = lax.ppermute(state, "tm", [(steps - n, steps - n - 1)])
        if n == steps // 2:
            gain = gain_rows(cross[0], w)
            late, gain = lax.optimization_barrier((late, gain))
        (state,) = turn(n, mine, late, state, base, mean, w, packed)
    smoothed = lax.dynamic_slice(state[0], (first,), (MINE,))
    return (smoothed[None, :], gain[None, :, :])


def solution(mesh):
    in_specs = (
        P("tm", "row", None),
        P("tm", "row", None),
        P("tm", "row"),
        P("tm", "row"),
        P("row"),
    )
    out_specs = (P("tm", "row"), P("tm", "row", None))
    return jax.shard_map(
        per_device, mesh=mesh, in_specs=in_specs, out_specs=out_specs, check_vma=False
    )
```

```python
import functools

import jax
import jax.numpy as jnp
from jax import lax
from jax.experimental import pallas as pl
from jax.experimental.pallas import tpu as pltpu
from jax.sharding import PartitionSpec as P

f32, bf16 = jnp.float32, jnp.bfloat16
N, LANES = 1536, 128
MINE = 48
PIECE = 4 * MINE
B = 2 * PIECE
H = 128
TILE = 512
Y, Z = 4, 8
VMEM_WHOLE = pl.BlockSpec(memory_space=pltpu.VMEM)
SMEM_WHOLE = pl.BlockSpec(memory_space=pltpu.SMEM)

def inv4(d):
    a,b,c=d[0][0],d[1][0],d[1][1]
    r=1.0/(a*c-b*b)
    p,q,s=c*r,-b*r,a*r
    e0,e1,g0,g1=d[2][0],d[2][1],d[3][0],d[3][1]
    x00,x01=e0*p+e1*q,e0*q+e1*s
    x10,x11=g0*p+g1*q,g0*q+g1*s
    u=d[2][2]-(x00*e0+x01*e1)
    v=d[3][2]-(x10*e0+x11*e1)
    w=d[3][3]-(x10*g0+x11*g1)
    r2=1.0/(u*w-v*v)
    U,V,W=w*r2,-v*r2,u*r2
    y00,y01=U*x00+V*x10,U*x01+V*x11
    y10,y11=V*x00+W*x10,V*x01+W*x11
    i00=p+x00*y00+x10*y10
    i01=q+x00*y01+x10*y11
    i11=s+x01*y01+x11*y11
    return [[i00,i01,-y00,-y10],[i01,i11,-y01,-y11],[-y00,-y01,U,V],[-y10,-y11,V,W]]


def product(a, b):
    return [[sum(x[k] * b[k][j] for k in range(4)) for j in range(4)] for x in a]


def inv8(d):
    a = inv4(d[:4])
    e = [row[:4] for row in d[4:]]
    x = product(e, a)
    s = [[d[4 + i][4 + j] - sum(x[i][k] * e[j][k] for k in range(4)) for j in range(i + 1)] for i in range(4)]
    w = inv4(s)
    y = product(w, x)
    top = [[None] * 4 for _ in range(4)]
    for i in range(4):
        for j in range(i + 1):
            top[i][j] = top[j][i] = a[i][j] + sum(x[k][i] * y[k][j] for k in range(4))
    upper = [top[i] + [-y[k][i] for k in range(4)] for i in range(4)]
    return upper + [[-v for v in y[i]] + w[i] for i in range(4)]


def leaf(m_ref):
    k, rows = 8, H // 8
    full = lambda x: jnp.broadcast_to(x, (k, H))
    lane = lax.broadcasted_iota(jnp.int32, (k, H), 1)
    sub = lax.broadcasted_iota(jnp.int32, (k, H), 0)
    m = [m_ref[k * v : k * v + k, :] for v in range(rows)]
    for p in range(rows):
        o = p * k
        r = [full(m[p][i : i + 1, :]) for i in range(k)]
        d = [[full(r[i][:, o + j : o + j + 1]) for j in range(i + 1)] for i in range(k)]
        inverse = inv8(d)
        pivots = (lane >= o) & (lane < o + k)
        r = [jnp.where(lane == o + i, -1.0, jnp.where(pivots, 0.0, r[i])) for i in range(k)]
        t = [sum(inverse[i][j] * r[j] for j in range(k)) for i in range(k)]
        new = list(m)
        for v in [(p + 1 + n) % rows for n in range(rows - 1)]:
            x = jnp.where(pivots, 0.0, m[v])
            for q in range(k):
                x = x - full(m[v][:, o + q : o + q + 1]) * t[q]
            new[v] = x
        new[p] = t[0]
        for i in range(1, k):
            new[p] = jnp.where(sub == i, t[i], new[p])
        m = new
    for v in range(rows):
        m_ref[k * v : k * v + k, :] = m[v]


def split(x):
    h = x.astype(bf16)
    return h, (x - h.astype(f32)).astype(bf16)


def wide(x):
    h, l = split(x)
    return jnp.concatenate([h, h, l], 1)


def tall(x):
    h, l = split(x)
    return jnp.concatenate([h, l, h], 0)


def dot(a, b):
    return jnp.dot(a, b, preferred_element_type=f32)


def block_sweep(d_ref, m_ref, r_ref, odd=0, first_ref=None):
    def step(k, _):
        o = pl.multiple_of(jnp.where(odd > 0, B // H - 1 - k, k) * H, H)

        def sweep_leaf():
            m_ref[...] = d_ref[pl.ds(o, H), pl.ds(o, H)]
            leaf(m_ref)

        if first_ref is None:
            sweep_leaf()
        else:
            pl.when(k > 0)(sweep_leaf)

            @pl.when(k == 0)
            def _():
                m_ref[...] = first_ref[...]

        minus = m_ref[...]
        t = -dot(wide(minus), tall(d_ref[pl.ds(o, H), :]))
        c = wide(d_ref[:, pl.ds(o, H)])
        r_ref[...] = -dot(c, tall(minus))
        d_ref[...] = d_ref[...] - dot(c, tall(t))
        d_ref[pl.ds(o, H), :] = t
        d_ref[:, pl.ds(o, H)] = r_ref[...]
        d_ref[pl.ds(o, H), pl.ds(o, H)] = minus
        return 0

    lax.fori_loop(0, B // H, step, 0)


def stage_kernel(stage, ids, near_ref, far_ref, *refs):
    first_ref, *refs = refs
    last = stage == N // B - 1
    if last:
        w_ref, out_ref, p_ref, t3_ref, d_ref, m_ref, r_ref, sems = refs
    else:
        w_ref, p_ref, t3_ref, d_ref, m_ref, r_ref = refs

    def leave(j):
        there = pl.ds(pl.multiple_of(ids[j] * B, B), B)
        return pltpu.make_async_copy(w_ref.at[there, :], out_ref.at[there, :], sems.at[j])

    here = pl.multiple_of(ids[stage] * B, B)
    for n, ref in enumerate((near_ref, far_ref)):
        z = ids[4 + n]
        for d in range(Y):
            y = lax.rem(ids[6] + d, Y)
            to = pl.multiple_of(lax.rem(z, 2) * PIECE + y * MINE, 16)
            p_ref[pl.ds(to, MINE), :] = ref[d * MINE : (d + 1) * MINE, :]
    rows = pl.ds(here, B)
    w_ref[rows, :] = p_ref[...].astype(f32)
    if stage:

        def clear(j, _):
            w_ref[rows, pl.ds(pl.multiple_of(ids[j] * B, B), B)] = jnp.zeros((B, B), f32)
            return 0

        lax.fori_loop(0, stage, clear, 0)

        def earlier(j, _):
            there = pl.multiple_of(ids[j] * B, B)
            p = p_ref[:, pl.ds(there, B)]
            p = jnp.concatenate([p, p], 1)

            def tile(n, _):
                q = pl.ds(pl.multiple_of(n * TILE, TILE), TILE)
                h, l = split(w_ref[pl.ds(there, B), q])
                w_ref[rows, q] = w_ref[rows, q] - dot(p, jnp.concatenate([h, l], 0))
                return 0

            return lax.fori_loop(0, N // TILE, tile, 0)

        lax.fori_loop(0, stage, earlier, 0)
    d_ref[...] = w_ref[rows, pl.ds(here, B)]
    if stage:
        block_sweep(d_ref, m_ref, r_ref)
    else:
        block_sweep(d_ref, m_ref, r_ref, ids[7], first_ref)
    minus = d_ref[...]
    left = wide(minus)

    def forward(n, _):
        q = pl.ds(pl.multiple_of(n * TILE, TILE), TILE)
        t = -dot(left, tall(w_ref[rows, q]))
        t3_ref[:, q] = tall(t)
        w_ref[rows, q] = t
        return 0

    lax.fori_loop(0, N // TILE, forward, 0)
    w_ref[rows, pl.ds(here, B)] = minus
    if last:
        leave(stage).start()
    if stage:

        def update(j, _):
            back = pl.ds(pl.multiple_of(ids[j] * B, B), B)
            c = wide(w_ref[back, pl.ds(here, B)])
            d_ref[...] = -dot(c, tall(minus))

            def tile(n, _):
                q = pl.ds(pl.multiple_of(n * TILE, TILE), TILE)
                w_ref[back, q] = w_ref[back, q] - dot(c, t3_ref[:, q])
                return 0

            lax.fori_loop(0, N // TILE, tile, 0)
            w_ref[back, pl.ds(here, B)] = d_ref[...]
            if last:
                leave(j).start()
            return 0

        lax.fori_loop(0, stage, update, 0)
    if last:
        for j in range(N // B):
            leave(j).wait()


def gain_kernel(cross_ref, w_ref, g_ref):
    c3 = wide(cross_ref[...])

    def gains(j, _):
        q = pl.ds(pl.multiple_of(j * B, B), B)
        g_ref[:, q] = -dot(c3, tall(w_ref[:, q]))
        return 0

    lax.fori_loop(0, N // B, gains, 0)


def gain_rows(cross, minus_inverse):
    return pl.pallas_call(
        gain_kernel,
        name="gains",
        out_shape=jax.ShapeDtypeStruct(cross.shape, f32),
        in_specs=[VMEM_WHOLE] * 2,
        out_specs=VMEM_WHOLE,
        compiler_params=pltpu.CompilerParams(vmem_limit_bytes=12 << 20),
        cost_estimate=pl.CostEstimate(flops=1_000_000_000, bytes_accessed=4 * N * N, transcendentals=0),
    )(cross, minus_inverse)


def first_leaf_kernel(ids, own_ref, m_ref, n_ref):
    odd = ids[7]
    lanes = pl.ds(pl.multiple_of(ids[0] * B + odd * (B - H), H), H)
    for d in range(Y):
        to = pl.multiple_of(lax.rem(ids[6] + d, Y) * MINE, 16)
        n_ref[pl.ds(to, MINE), :] = own_ref[d * MINE : (d + 1) * MINE, lanes]
    m_ref[...] = n_ref[pl.ds(pl.multiple_of(odd * (PIECE - H), 16), H), :].astype(f32)
    leaf(m_ref)


def first_leaf(ids, own):
    return pl.pallas_call(
        first_leaf_kernel,
        name="first_leaf",
        out_shape=jax.ShapeDtypeStruct((H, H), f32),
        in_specs=[SMEM_WHOLE, VMEM_WHOLE],
        out_specs=VMEM_WHOLE,
        scratch_shapes=[pltpu.VMEM((PIECE, H), bf16)],
        compiler_params=pltpu.CompilerParams(vmem_limit_bytes=4 << 20),
        cost_estimate=pl.CostEstimate(flops=6_000_000_000, bytes_accessed=2 * PIECE * N, transcendentals=0),
    )(ids, own)


def sweep_stage(stage, ids, near, far, other):
    last = stage == N // B - 1
    outs = pl.pallas_call(
        functools.partial(stage_kernel, stage),
        name="stage" + str(stage),
        out_shape=[jax.ShapeDtypeStruct((N, N), f32)] * (1 + last),
        in_specs=[SMEM_WHOLE] + [VMEM_WHOLE] * 3,
        out_specs=[VMEM_WHOLE] + [pl.BlockSpec(memory_space=pltpu.HBM)] * last,
        scratch_shapes=[
            pltpu.VMEM((B, N), bf16),
            pltpu.VMEM((3 * B, N), bf16),
            pltpu.VMEM((B, B), f32),
            pltpu.VMEM((H, H), f32),
            pltpu.VMEM((B, H), f32),
        ]
        + [pltpu.SemaphoreType.DMA((N // B,))] * last,
        input_output_aliases={3: 0} if stage else {},
        compiler_params=pltpu.CompilerParams(vmem_limit_bytes=(38 if last else 24) << 20),
        cost_estimate=pl.CostEstimate(flops=40_000_000_000, bytes_accessed=4 * B * N, transcendentals=0),
    )(ids, near, far, other)
    return outs[-1]


def matvec(m_ref, v_ref, out_ref):
    for i in range(N // LANES):
        rows = slice(i * LANES, (i + 1) * LANES)
        total = m_ref[rows, :LANES] * v_ref[:, :LANES]
        for j in range(1, N // LANES):
            lanes = slice(j * LANES, (j + 1) * LANES)
            total = total + m_ref[rows, lanes] * v_ref[:, lanes]
        out_ref[:, rows] = jnp.sum(total.T, axis=0, keepdims=True)


def turn_kernel(n, mine_ref, *refs):
    if n:
        late_ref, before_ref, base_ref, mean_ref, w_ref, x_ref, s_ref, v_ref, y_ref = refs
    else:
        w_ref, x_ref, s_ref, base_ref, mean_ref, v_ref, y_ref = refs
        for j in range(N // LANES):
            rows = slice(j * LANES, (j + 1) * LANES)
            vectors = x_ref[rows, N:].T[:8, :]
            mean_ref[:, rows] = vectors[0:1]
            base_ref[:, rows] = jnp.where(mine_ref[0] == 0, vectors[2:3], 0.0) - vectors[1:2]

    @pl.when(mine_ref[0] == n)
    def _():
        v_ref[...] = late_ref[...] + base_ref[...] if n else base_ref[...]
        matvec(w_ref, v_ref, y_ref)
        matvec(x_ref, y_ref, s_ref)
        s_ref[...] = mean_ref[...] - s_ref[...]

    @pl.when(mine_ref[0] != n)
    def _():
        s_ref[...] = before_ref[...] if n else mean_ref[...]


def turn(n, mine, *args):
    return pl.pallas_call(
        functools.partial(turn_kernel, n),
        name="turn" + str(n),
        out_shape=[jax.ShapeDtypeStruct((1, N), f32)] * (1 if n else 3),
        in_specs=[SMEM_WHOLE] + [VMEM_WHOLE] * len(args),
        out_specs=[VMEM_WHOLE] * (1 if n else 3),
        scratch_shapes=[pltpu.VMEM((1, N), f32), pltpu.VMEM((1, N), f32)],
        compiler_params=pltpu.CompilerParams(vmem_limit_bytes=4 << 20),
        cost_estimate=pl.CostEstimate(flops=4 * N * N, bytes_accessed=8 * N * N, transcendentals=0),
    )(mine, *args)


def swap(x, inner):
    pairs = []
    for z in range(Z):
        other = z ^ 1 if inner else (z + (1 if z % 2 else -1)) % Z
        pairs += [(z * Y + y, other * Y + y) for y in range(Y)]
    return lax.ppermute(x, "row", pairs)


def along_y(x, d):
    return lax.ppermute(x, "row", [(z * Y + (y + d) % Y, z * Y + y) for z in range(Z) for y in range(Y)])


def per_device(pred_cov, cross, filt_mean, pred_mean, next_smoothed):
    steps = lax.axis_size("tm")
    row = lax.axis_index("row")
    y, z = row % Y, row // Y
    columns = jnp.stack([filt_mean[0], pred_mean[0], next_smoothed], axis=1)
    packed = jnp.concatenate([cross[0], jnp.pad(columns, ((0, 0), (0, LANES - 3)))], axis=1)
    first = (row * MINE).astype(jnp.uint32)
    mine = (steps - 1 - lax.axis_index("tm")).astype(jnp.int32)[None]
    pred_cov, first, mine = lax.optimization_barrier((pred_cov, first, mine))

    own = jnp.concatenate([pred_cov[0]] + [along_y(pred_cov[0], d) for d in range(1, Y)], axis=0)
    packed, own = lax.optimization_barrier((packed, own))
    packed = lax.all_gather(packed, "row", axis=0, tiled=True)
    a1, b1 = swap(own, True), swap(own, False)
    a2, b2 = swap(b1, True), swap(a1, False)
    a3, b3 = swap(b2, True), swap(a2, False)
    b4 = swap(a3, False)
    e = 1 - 2 * (z % 2)
    at = lambda k: (z + e * k + Z) % Z
    order = [at(0) // 2, at(-1) // 2, at(2) // 2, at(-3) // 2]
    ids = lambda m, n: jnp.stack(order + [at(m), at(n), y, z % 2]).astype(jnp.int32)
    w = sweep_stage(0, ids(0, 1), own, a1, first_leaf(ids(0, 1), own))
    w = sweep_stage(1, ids(-1, -2), b1, b2, w)
    w = sweep_stage(2, ids(2, 3), a2, a3, w)
    w = sweep_stage(3, ids(-3, -4), b3, b4, w)

    state, base, mean = turn(0, mine, w, packed)
    for n in range(1, steps):
        late = lax.ppermute(state, "tm", [(steps - n, steps - n - 1)])
        if n == steps // 2:
            gain = gain_rows(cross[0], w)
            late, gain = lax.optimization_barrier((late, gain))
        (state,) = turn(n, mine, late, state, base, mean, w, packed)
    smoothed = lax.dynamic_slice(state[0], (first,), (MINE,))
    return (smoothed[None, :], gain[None, :, :])


def solution(mesh):
    in_specs = (
        P("tm", "row", None),
        P("tm", "row", None),
        P("tm", "row"),
        P("tm", "row"),
        P("row"),
    )
    out_specs = (P("tm", "row"), P("tm", "row", None))
    return jax.shard_map(
        per_device, mesh=mesh, in_specs=in_specs, out_specs=out_specs, check_vma=False
    )
```

```python
import functools

import jax
import jax.numpy as jnp
from jax import lax
from jax.experimental import pallas as pl
from jax.experimental.pallas import tpu as pltpu
from jax.sharding import PartitionSpec as P

f32, bf16 = jnp.float32, jnp.bfloat16
N, LANES = 1536, 128
MINE = 48
PIECE = 4 * MINE
B = 2 * PIECE
H = 128
TILE = 1536
Y, Z = 4, 8
VMEM_WHOLE = pl.BlockSpec(memory_space=pltpu.VMEM)
SMEM_WHOLE = pl.BlockSpec(memory_space=pltpu.SMEM)

def inv4(d):
    a,b,c=d[0][0],d[1][0],d[1][1]
    r=1.0/(a*c-b*b)
    p,q,s=c*r,-b*r,a*r
    e0,e1,g0,g1=d[2][0],d[2][1],d[3][0],d[3][1]
    x00,x01=e0*p+e1*q,e0*q+e1*s
    x10,x11=g0*p+g1*q,g0*q+g1*s
    u=d[2][2]-(x00*e0+x01*e1)
    v=d[3][2]-(x10*e0+x11*e1)
    w=d[3][3]-(x10*g0+x11*g1)
    r2=1.0/(u*w-v*v)
    U,V,W=w*r2,-v*r2,u*r2
    y00,y01=U*x00+V*x10,U*x01+V*x11
    y10,y11=V*x00+W*x10,V*x01+W*x11
    i00=p+x00*y00+x10*y10
    i01=q+x00*y01+x10*y11
    i11=s+x01*y01+x11*y11
    return [[i00,i01,-y00,-y10],[i01,i11,-y01,-y11],[-y00,-y01,U,V],[-y10,-y11,V,W]]


def product(a, b):
    return [[sum(x[k] * b[k][j] for k in range(4)) for j in range(4)] for x in a]


def inv8(d):
    a = inv4(d[:4])
    e = [row[:4] for row in d[4:]]
    x = product(e, a)
    s = [[d[4 + i][4 + j] - sum(x[i][k] * e[j][k] for k in range(4)) for j in range(i + 1)] for i in range(4)]
    w = inv4(s)
    y = product(w, x)
    top = [[None] * 4 for _ in range(4)]
    for i in range(4):
        for j in range(i + 1):
            top[i][j] = top[j][i] = a[i][j] + sum(x[k][i] * y[k][j] for k in range(4))
    upper = [top[i] + [-y[k][i] for k in range(4)] for i in range(4)]
    return upper + [[-v for v in y[i]] + w[i] for i in range(4)]


def leaf(m_ref):
    k, rows = 8, H // 8
    full = lambda x: jnp.broadcast_to(x, (k, H))
    lane = lax.broadcasted_iota(jnp.int32, (k, H), 1)
    sub = lax.broadcasted_iota(jnp.int32, (k, H), 0)
    m = [m_ref[k * v : k * v + k, :] for v in range(rows)]
    for p in range(rows):
        o = p * k
        r = [full(m[p][i : i + 1, :]) for i in range(k)]
        d = [[full(r[i][:, o + j : o + j + 1]) for j in range(i + 1)] for i in range(k)]
        inverse = inv8(d)
        pivots = (lane >= o) & (lane < o + k)
        r = [jnp.where(lane == o + i, -1.0, jnp.where(pivots, 0.0, r[i])) for i in range(k)]
        t = [sum(inverse[i][j] * r[j] for j in range(k)) for i in range(k)]
        new = list(m)
        for v in [(p + 1 + n) % rows for n in range(rows - 1)]:
            x = jnp.where(pivots, 0.0, m[v])
            for q in range(k):
                x = x - full(m[v][:, o + q : o + q + 1]) * t[q]
            new[v] = x
        new[p] = t[0]
        for i in range(1, k):
            new[p] = jnp.where(sub == i, t[i], new[p])
        m = new
    for v in range(rows):
        m_ref[k * v : k * v + k, :] = m[v]


def split(x):
    h = x.astype(bf16)
    return h, (x - h.astype(f32)).astype(bf16)


def wide(x):
    h, l = split(x)
    return jnp.concatenate([h, h, l], 1)


def tall(x):
    h, l = split(x)
    return jnp.concatenate([h, l, h], 0)


def dot(a, b):
    return jnp.dot(a, b, preferred_element_type=f32)


def block_sweep(d_ref, m_ref, r_ref, odd=0, first_ref=None):
    def step(k, _):
        o = pl.multiple_of(jnp.where(odd > 0, B // H - 1 - k, k) * H, H)

        def sweep_leaf():
            m_ref[...] = d_ref[pl.ds(o, H), pl.ds(o, H)]
            leaf(m_ref)

        if first_ref is None:
            sweep_leaf()
        else:
            pl.when(k > 0)(sweep_leaf)

            @pl.when(k == 0)
            def _():
                m_ref[...] = first_ref[...]

        minus = m_ref[...]
        t = -dot(wide(minus), tall(d_ref[pl.ds(o, H), :]))
        c = wide(d_ref[:, pl.ds(o, H)])
        r_ref[...] = -dot(c, tall(minus))
        d_ref[...] = d_ref[...] - dot(c, tall(t))
        d_ref[pl.ds(o, H), :] = t
        d_ref[:, pl.ds(o, H)] = r_ref[...]
        d_ref[pl.ds(o, H), pl.ds(o, H)] = minus
        return 0

    lax.fori_loop(0, B // H, step, 0)


def stage_kernel(stage, ids, near_ref, far_ref, *refs):
    first_ref, *refs = refs
    last = stage == N // B - 1
    if last:
        w_ref, out_ref, p_ref, t3_ref, d_ref, m_ref, r_ref, sems = refs
    else:
        w_ref, p_ref, t3_ref, d_ref, m_ref, r_ref = refs

    def leave(j):
        there = pl.ds(pl.multiple_of(ids[j] * B, B), B)
        return pltpu.make_async_copy(w_ref.at[there, :], out_ref.at[there, :], sems.at[j])

    here = pl.multiple_of(ids[stage] * B, B)
    for n, ref in enumerate((near_ref, far_ref)):
        z = ids[4 + n]
        for d in range(Y):
            y = lax.rem(ids[6] + d, Y)
            to = pl.multiple_of(lax.rem(z, 2) * PIECE + y * MINE, 16)
            p_ref[pl.ds(to, MINE), :] = ref[d * MINE : (d + 1) * MINE, :]
    rows = pl.ds(here, B)
    w_ref[rows, :] = p_ref[...].astype(f32)
    if stage:

        def clear(j, _):
            w_ref[rows, pl.ds(pl.multiple_of(ids[j] * B, B), B)] = jnp.zeros((B, B), f32)
            return 0

        lax.fori_loop(0, stage, clear, 0)

        def earlier(j, _):
            there = pl.multiple_of(ids[j] * B, B)
            p = p_ref[:, pl.ds(there, B)]
            p = jnp.concatenate([p, p], 1)

            def tile(n, _):
                q = pl.ds(pl.multiple_of(n * TILE, TILE), TILE)
                h, l = split(w_ref[pl.ds(there, B), q])
                w_ref[rows, q] = w_ref[rows, q] - dot(p, jnp.concatenate([h, l], 0))
                return 0

            return lax.fori_loop(0, N // TILE, tile, 0)

        lax.fori_loop(0, stage, earlier, 0)
    d_ref[...] = w_ref[rows, pl.ds(here, B)]
    if stage:
        block_sweep(d_ref, m_ref, r_ref)
    else:
        block_sweep(d_ref, m_ref, r_ref, ids[7], first_ref)
    minus = d_ref[...]
    left = wide(minus)

    def forward(n, _):
        q = pl.ds(pl.multiple_of(n * TILE, TILE), TILE)
        t = -dot(left, tall(w_ref[rows, q]))
        t3_ref[:, q] = tall(t)
        w_ref[rows, q] = t
        return 0

    lax.fori_loop(0, N // TILE, forward, 0)
    w_ref[rows, pl.ds(here, B)] = minus
    if last:
        leave(stage).start()
    if stage:

        def update(j, _):
            back = pl.ds(pl.multiple_of(ids[j] * B, B), B)
            c = wide(w_ref[back, pl.ds(here, B)])
            d_ref[...] = -dot(c, tall(minus))

            def tile(n, _):
                q = pl.ds(pl.multiple_of(n * TILE, TILE), TILE)
                w_ref[back, q] = w_ref[back, q] - dot(c, t3_ref[:, q])
                return 0

            lax.fori_loop(0, N // TILE, tile, 0)
            w_ref[back, pl.ds(here, B)] = d_ref[...]
            if last:
                leave(j).start()
            return 0

        lax.fori_loop(0, stage, update, 0)
    if last:
        for j in range(N // B):
            leave(j).wait()


def gain_kernel(cross_ref, w_ref, g_ref):
    c3 = wide(cross_ref[...])

    def gains(j, _):
        q = pl.ds(pl.multiple_of(j * B, B), B)
        g_ref[:, q] = -dot(c3, tall(w_ref[:, q]))
        return 0

    lax.fori_loop(0, N // B, gains, 0)


def gain_rows(cross, minus_inverse):
    return pl.pallas_call(
        gain_kernel,
        name="gains",
        out_shape=jax.ShapeDtypeStruct(cross.shape, f32),
        in_specs=[VMEM_WHOLE] * 2,
        out_specs=VMEM_WHOLE,
        compiler_params=pltpu.CompilerParams(vmem_limit_bytes=12 << 20),
        cost_estimate=pl.CostEstimate(flops=1_000_000_000, bytes_accessed=4 * N * N, transcendentals=0),
    )(cross, minus_inverse)


def first_leaf_kernel(ids, own_ref, m_ref, n_ref):
    odd = ids[7]
    lanes = pl.ds(pl.multiple_of(ids[0] * B + odd * (B - H), H), H)
    for d in range(Y):
        to = pl.multiple_of(lax.rem(ids[6] + d, Y) * MINE, 16)
        n_ref[pl.ds(to, MINE), :] = own_ref[d * MINE : (d + 1) * MINE, lanes]
    m_ref[...] = n_ref[pl.ds(pl.multiple_of(odd * (PIECE - H), 16), H), :].astype(f32)
    leaf(m_ref)


def first_leaf(ids, own):
    return pl.pallas_call(
        first_leaf_kernel,
        name="first_leaf",
        out_shape=jax.ShapeDtypeStruct((H, H), f32),
        in_specs=[SMEM_WHOLE, VMEM_WHOLE],
        out_specs=VMEM_WHOLE,
        scratch_shapes=[pltpu.VMEM((PIECE, H), bf16)],
        compiler_params=pltpu.CompilerParams(vmem_limit_bytes=4 << 20),
        cost_estimate=pl.CostEstimate(flops=6_000_000_000, bytes_accessed=2 * PIECE * N, transcendentals=0),
    )(ids, own)


def sweep_stage(stage, ids, near, far, other):
    last = stage == N // B - 1
    outs = pl.pallas_call(
        functools.partial(stage_kernel, stage),
        name="stage" + str(stage),
        out_shape=[jax.ShapeDtypeStruct((N, N), f32)] * (1 + last),
        in_specs=[SMEM_WHOLE] + [VMEM_WHOLE] * 3,
        out_specs=[VMEM_WHOLE] + [pl.BlockSpec(memory_space=pltpu.HBM)] * last,
        scratch_shapes=[
            pltpu.VMEM((B, N), bf16),
            pltpu.VMEM((3 * B, N), bf16),
            pltpu.VMEM((B, B), f32),
            pltpu.VMEM((H, H), f32),
            pltpu.VMEM((B, H), f32),
        ]
        + [pltpu.SemaphoreType.DMA((N // B,))] * last,
        input_output_aliases={3: 0} if stage else {},
        compiler_params=pltpu.CompilerParams(vmem_limit_bytes=(38 if last else 24) << 20),
        cost_estimate=pl.CostEstimate(flops=40_000_000_000, bytes_accessed=4 * B * N, transcendentals=0),
    )(ids, near, far, other)
    return outs[-1]


def matvec(m_ref, v_ref, out_ref):
    for i in range(N // LANES):
        rows = slice(i * LANES, (i + 1) * LANES)
        total = m_ref[rows, :LANES] * v_ref[:, :LANES]
        for j in range(1, N // LANES):
            lanes = slice(j * LANES, (j + 1) * LANES)
            total = total + m_ref[rows, lanes] * v_ref[:, lanes]
        out_ref[:, rows] = jnp.sum(total.T, axis=0, keepdims=True)


def turn_kernel(n, mine_ref, *refs):
    if n:
        late_ref, before_ref, base_ref, mean_ref, w_ref, x_ref, s_ref, v_ref, y_ref = refs
    else:
        w_ref, x_ref, s_ref, base_ref, mean_ref, v_ref, y_ref = refs
        for j in range(N // LANES):
            rows = slice(j * LANES, (j + 1) * LANES)
            vectors = x_ref[rows, N:].T[:8, :]
            mean_ref[:, rows] = vectors[0:1]
            base_ref[:, rows] = jnp.where(mine_ref[0] == 0, vectors[2:3], 0.0) - vectors[1:2]

    @pl.when(mine_ref[0] == n)
    def _():
        v_ref[...] = late_ref[...] + base_ref[...] if n else base_ref[...]
        matvec(w_ref, v_ref, y_ref)
        matvec(x_ref, y_ref, s_ref)
        s_ref[...] = mean_ref[...] - s_ref[...]

    @pl.when(mine_ref[0] != n)
    def _():
        s_ref[...] = before_ref[...] if n else mean_ref[...]


def turn(n, mine, *args):
    return pl.pallas_call(
        functools.partial(turn_kernel, n),
        name="turn" + str(n),
        out_shape=[jax.ShapeDtypeStruct((1, N), f32)] * (1 if n else 3),
        in_specs=[SMEM_WHOLE] + [VMEM_WHOLE] * len(args),
        out_specs=[VMEM_WHOLE] * (1 if n else 3),
        scratch_shapes=[pltpu.VMEM((1, N), f32), pltpu.VMEM((1, N), f32)],
        compiler_params=pltpu.CompilerParams(vmem_limit_bytes=4 << 20),
        cost_estimate=pl.CostEstimate(flops=4 * N * N, bytes_accessed=8 * N * N, transcendentals=0),
    )(mine, *args)


def swap(x, inner):
    pairs = []
    for z in range(Z):
        other = z ^ 1 if inner else (z + (1 if z % 2 else -1)) % Z
        pairs += [(z * Y + y, other * Y + y) for y in range(Y)]
    return lax.ppermute(x, "row", pairs)


def along_y(x, d):
    return lax.ppermute(x, "row", [(z * Y + (y + d) % Y, z * Y + y) for z in range(Z) for y in range(Y)])


def per_device(pred_cov, cross, filt_mean, pred_mean, next_smoothed):
    steps = lax.axis_size("tm")
    row = lax.axis_index("row")
    y, z = row % Y, row // Y
    columns = jnp.stack([filt_mean[0], pred_mean[0], next_smoothed], axis=1)
    packed = jnp.concatenate([cross[0], jnp.pad(columns, ((0, 0), (0, LANES - 3)))], axis=1)
    first = (row * MINE).astype(jnp.uint32)
    mine = (steps - 1 - lax.axis_index("tm")).astype(jnp.int32)[None]
    pred_cov, first, mine = lax.optimization_barrier((pred_cov, first, mine))

    own = jnp.concatenate([pred_cov[0]] + [along_y(pred_cov[0], d) for d in range(1, Y)], axis=0)
    packed, own = lax.optimization_barrier((packed, own))
    packed = lax.all_gather(packed, "row", axis=0, tiled=True)
    a1, b1 = swap(own, True), swap(own, False)
    a2, b2 = swap(b1, True), swap(a1, False)
    a3, b3 = swap(b2, True), swap(a2, False)
    b4 = swap(a3, False)
    e = 1 - 2 * (z % 2)
    at = lambda k: (z + e * k + Z) % Z
    order = [at(0) // 2, at(-1) // 2, at(2) // 2, at(-3) // 2]
    ids = lambda m, n: jnp.stack(order + [at(m), at(n), y, z % 2]).astype(jnp.int32)
    w = sweep_stage(0, ids(0, 1), own, a1, first_leaf(ids(0, 1), own))
    w = sweep_stage(1, ids(-1, -2), b1, b2, w)
    w = sweep_stage(2, ids(2, 3), a2, a3, w)
    w = sweep_stage(3, ids(-3, -4), b3, b4, w)

    state, base, mean = turn(0, mine, w, packed)
    for n in range(1, steps):
        late = lax.ppermute(state, "tm", [(steps - n, steps - n - 1)])
        if n == steps // 2:
            gain = gain_rows(cross[0], w)
            late, gain = lax.optimization_barrier((late, gain))
        (state,) = turn(n, mine, late, state, base, mean, w, packed)
    smoothed = lax.dynamic_slice(state[0], (first,), (MINE,))
    return (smoothed[None, :], gain[None, :, :])


def solution(mesh):
    in_specs = (
        P("tm", "row", None),
        P("tm", "row", None),
        P("tm", "row"),
        P("tm", "row"),
        P("row"),
    )
    out_specs = (P("tm", "row"), P("tm", "row", None))
    return jax.shard_map(
        per_device, mesh=mesh, in_specs=in_specs, out_specs=out_specs, check_vma=False
    )
```
